128 devices in a mesh: ctx: 32 (over z, x, core), head: 4 (over y).
Axes of the slice: x: 4, y: 4, z: 4, core: 2. Of those that a mesh axis runs over, the one named last changes fastest.
Arguments:
- queries: bfloat16 [16384, 4096], P('ctx', 'head'), may hold values from -8 to 8
- keys: bfloat16 [16384, 512], P('ctx', 'head'), may hold values from -8 to 8
- values: bfloat16 [16384, 512], P('ctx', 'head'), may hold values from -6 to 6
- distances: int32 [4, 3], P('head'), may hold values from 1 to 31, as said below
- out_weight: bfloat16 [4096, 2048], P('head'), may hold values from -0.09375 to 0.09375
- residual: bfloat16 [16384, 2048], P(('ctx', 'head')), may hold values from -6 to 6
- norm_gain: float32 [2048], replicated, may hold values from 0.25 to 1.75
- expert_gate_up: bfloat16 [128, 2048, 1536], P(('ctx', 'head')), may hold values from -0.125 to 0.125
- expert_down: bfloat16 [128, 768, 2048], P(('ctx', 'head')), may hold values from -0.21875 to 0.21875
- routes: int32 [16384, 8], P(('ctx', 'head')), may hold values from 0 to 127, all different within a row; in each aligned block of 128 rows (0 to 127, 128 to 255, ...) at most 16 rows name the same one
- route_weights: float32 [16384, 8], P(('ctx', 'head')), may hold values from 0.05 to 0.5
Outputs:
- attended: bfloat16 [16384, 2048], P(('ctx', 'head'))
- moe_out: bfloat16 [16384, 2048], P(('ctx', 'head'))
The draws below stay inside these ranges and needn't reach their ends.
Inputs may be any that keep to these rules, and one draw needn't show every extreme that they name: Each row holds 3 different distances; some row holds the distance 16384 // 1024. `routes`: among the 128 rows of one device, no expert is named by more than 16 rows.
All inputs are finite; a program needn't handle non-finite values.
Results may differ from the reference program's by a relative error of at most 0.01.
Values may be sent and summed in bfloat16 or wider, within the bound.
No kernel may reach another device: no remote copies, remote signals or barrier semaphores. Data moves between devices by JAX's collectives and lax.ppermute only.
A program may use at most 128 MiB of HBM per device.

```python
import math
import jax
import jax.numpy as jnp
import numpy as np
from jax import lax

D = 2048
Q_HEADS = 32
KV_HEADS = 4
HD = 128
FFE = 768
TOP = 8
BLK = 128
DIST = 3
TOK_DEV = 512
TOKENS = 16384
TOK_LOC = 128
EXPERTS = 128
CAP = 16


def draw_queries(key, part):
    result = jnp.clip(jax.random.normal(jax.random.fold_in(key, 11), (TOKENS, Q_HEADS * HD), jnp.float32), -6.0, 6.0)
    return result.astype(jnp.bfloat16)


def draw_keys(key, part):
    result = jnp.clip(jax.random.normal(jax.random.fold_in(key, 12), (TOKENS, KV_HEADS * HD), jnp.float32), -6.0, 6.0)
    return result.astype(jnp.bfloat16)


def draw_distances(key, part):
    shards = TOKENS // TOK_DEV
    middle = shards // 2
    chosen = jax.random.randint(jax.random.fold_in(key, 299), (), 0, KV_HEADS)
    rows = []
    for head in range(KV_HEADS):
        others = jax.random.permutation(jax.random.fold_in(key, 300 + head), shards - 2)[:DIST] + 1
        others = jnp.where(others >= middle, others + 1, others)
        mixed_row = jnp.where((jnp.arange(DIST) == 0) & (chosen == head), middle, others)
        rows.append(mixed_row)
    return jnp.stack(rows).astype(jnp.int32)


def levels(key, shape, pieces, least, largest):
    factor_of = 1.0
    for axis_at, shards_of in pieces:
        heights = jax.random.uniform(jax.random.fold_in(jax.random.fold_in(key, 6), axis_at), (shards_of,), jnp.float32, least / len(pieces), largest / len(pieces))
        factor_of = factor_of * jnp.repeat(jnp.exp(heights), shape[axis_at] // shards_of).reshape((-1,) + (1,) * (len(shape) - 1 - axis_at))
    return factor_of


def deal_out(stream_key, own, number, rows, number_of, top, most, skew):
    ranking = jax.random.permutation(stream_key, number_of)
    heavy_load, usual = portions_of(number_of, rows * top, most, skew, True), portions_of(number_of, rows * top, most, skew, False)
    places = jnp.arange(number_of)

    def named(tallies, offset_by):
        used = int((tallies > 0).sum())
        fixed = max(1, used // 4)
        shifted = fixed + (places - fixed + offset_by * (used - fixed)) % max(1, number_of - fixed)
        return jnp.zeros((number_of,), jnp.int32).at[ranking[jnp.where(places < fixed, places, shifted)]].set(jnp.asarray(tallies, jnp.int32))

    tallies = jnp.where(number % 4 == 0, named(heavy_load, number // 4), named(usual, number - number // 4 - 1))
    mixed = jax.random.permutation(jax.random.fold_in(own, 3), number_of)
    source_of, sink = mixed[0:number_of // 2 * 2:2], mixed[1:number_of // 2 * 2:2]
    slack = jnp.minimum(tallies[source_of] - 1, most - tallies[sink]) // 2
    slack = jnp.where((source_of == ranking[0]) | (sink == ranking[0]) | (tallies[sink] == 0), 0, jnp.maximum(slack, 0))
    shifted = jax.random.randint(jax.random.fold_in(own, 4), (number_of // 2,), 0, 1 << 20) % (slack + 1)
    tallies = tallies.at[source_of].add(-shifted).at[sink].add(shifted)
    items = jnp.searchsorted(jnp.cumsum(tallies), jnp.arange(rows * top), side="right").astype(jnp.int32)
    listing = items.reshape(top, rows).T
    listing = listing[jax.random.permutation(jax.random.fold_in(own, 1), rows)]
    offset_by = jax.random.randint(jax.random.fold_in(own, 2), (rows, 1), 0, top)
    return jnp.take_along_axis(listing, (jnp.arange(top)[None, :] + offset_by) % top, axis=1)


def portions_of(number_of, total, bound, lean, full):
    weights = [(1 << 20) // math.isqrt(standing ** lean) + 1 for standing in range(1, number_of + 1)]
    largest = bound if full else min(bound, max(-(-total // number_of), total * weights[0] // sum(weights)))
    least = 1 if total - largest >= number_of - 1 else 0
    given, spare = [largest] + [least] * (number_of - 1), total - largest - least * (number_of - 1)
    while spare > 0:
        movable = [i for i in range(1, number_of) if given[i] < largest] or [i for i in range(1, number_of) if given[i] < bound]
        mass, remaining = sum([weights[i] for i in movable]), spare
        for i in movable:
            addition = min(bound - given[i], max(1, remaining * weights[i] // mass), spare)
            given[i] = given[i] + addition
            spare = spare - addition
    return np.array(given)


def scatter_about(key, shape, spread, bound, cuts=(), held_as=jnp.bfloat16):
    gain = levels(key, shape, cuts, -0.22, 0.18) if cuts else 1.0
    values = jax.random.normal(key, shape, jnp.float32) * spread * gain
    return jnp.minimum(jnp.maximum(values, -bound), bound).astype(held_as)


def setup_inputs(seed: int = 0) -> dict:
    key_list = jax.random.split(jax.random.key(seed), 12)
    queries = draw_queries(jax.random.fold_in(key_list[11], 71), 0)
    keys = draw_keys(jax.random.fold_in(key_list[11], 71), 0)
    values = scatter_about(key_list[2], (TOKENS, KV_HEADS * HD), 1.0, 6.0, ((0, 32), (1, 4)))
    distances = draw_distances(jax.random.fold_in(key_list[11], 71), 0)
    out_weight = scatter_about(key_list[4], (Q_HEADS * HD, D), (Q_HEADS * HD) ** -0.5, 0.09375, ((0, 4),))
    residual = scatter_about(key_list[5], (TOKENS, D), 1.0, 6.0, ((0, 128),))
    norm_gain = jnp.clip(1.0 + 0.15 * jax.random.normal(key_list[6], (D,), jnp.float32), 0.25, 1.75)
    expert_gate_up = scatter_about(key_list[7], (EXPERTS, D, 2 * FFE), D ** -0.5, 0.125, ((0, 128),))
    expert_down = scatter_about(key_list[8], (EXPERTS, FFE, D), FFE ** -0.5, 0.21875, ((0, 128),))
    routes_keys = jax.random.split(jax.random.fold_in(key_list[9], 1), TOKENS // TOK_LOC)
    routes_turns = jax.random.permutation(jax.random.fold_in(key_list[9], 3), TOKENS // TOK_LOC)
    routes = jax.vmap(lambda own, number: deal_out(jax.random.fold_in(key_list[9], 2), own, number, TOK_LOC, EXPERTS, TOP, CAP, 2))(routes_keys, routes_turns).reshape((TOKENS, TOP))
    route_weights = jnp.clip(jnp.exp(math.log(0.5) - 2.3025851 * jax.random.uniform(key_list[10], (TOKENS, TOP), jnp.float32) ** levels(key_list[10], (TOKENS, TOP), ((0, 128),), -0.2, 0.2)), 0.05, 0.5)
    return {"queries": queries, "keys": keys, "values": values, "distances": distances, "out_weight": out_weight, "residual": residual, "norm_gain": norm_gain, "expert_gate_up": expert_gate_up, "expert_down": expert_down, "routes": routes, "route_weights": route_weights}


def rounded(array):
    return lax.optimization_barrier(array.astype(jnp.bfloat16)).astype(jnp.float32)

def reference(queries, keys, values, distances, out_weight, residual, norm_gain, expert_gate_up, expert_down, routes, route_weights):
    groups = Q_HEADS // KV_HEADS
    shards = TOKENS // TOK_DEV
    blocks = TOK_DEV // BLK
    scale = 1.0 / math.sqrt(HD)
    query_all = queries.reshape(shards, TOK_DEV, KV_HEADS, groups, HD)
    key_all = keys.reshape(shards, TOK_DEV, KV_HEADS, HD)
    value_all = values.reshape(shards, TOK_DEV, KV_HEADS, HD)
    causal = jnp.arange(TOK_DEV)[:, None] >= jnp.arange(TOK_DEV)[None, :]
    head_index = jnp.arange(KV_HEADS, dtype=jnp.int32)[:, None]

    def one_shard(shard):
        query = query_all[shard].astype(jnp.float32)
        near_keys = key_all[shard].astype(jnp.float32)
        near_values = value_all[shard].astype(jnp.float32)
        local = jnp.einsum('tkgd,ukd->kgtu', query, near_keys) * scale
        local = jnp.where(causal, local, -jnp.inf)
        source = (shard - distances).astype(jnp.int32)
        usable = source >= 0
        clipped = jnp.maximum(source, 0).astype(jnp.int32)
        far_keys = key_all[clipped, :, head_index, :].astype(jnp.float32).reshape(KV_HEADS, DIST, blocks, BLK, HD)
        far_values = value_all[clipped, :, head_index, :].astype(jnp.float32).reshape(KV_HEADS, DIST, blocks, BLK, HD)
        query_blocks = query.reshape(blocks, BLK, KV_HEADS, groups, HD)
        remote = jnp.einsum('bqkgd,kjbud->kgjbqu', query_blocks, far_keys) * scale
        remote = jnp.where(usable[:, None, :, None, None, None], remote, -jnp.inf)
        highest = jnp.maximum(local.max(-1), remote.max(axis=(2, 5)).reshape(KV_HEADS, groups, TOK_DEV))
        near_weight = jnp.exp(local - highest[..., None])
        far_weight = jnp.exp(remote - highest.reshape(KV_HEADS, groups, blocks, BLK)[:, :, None, :, :, None])
        denominator = near_weight.sum(-1) + far_weight.sum(axis=(2, 5)).reshape(KV_HEADS, groups, TOK_DEV)
        mixed = jnp.einsum('kgtu,ukd->tkgd', rounded(near_weight), near_values)
        far_mixed = jnp.einsum('kgjbqu,kjbud->bqkgd', rounded(far_weight), far_values)
        mixed = mixed + far_mixed.reshape(TOK_DEV, KV_HEADS, groups, HD)
        mixed = mixed / jnp.transpose(denominator, (2, 0, 1))[..., None]
        return mixed.astype(jnp.bfloat16).reshape(TOK_DEV, Q_HEADS * HD)
    attention = lax.map(one_shard, jnp.arange(shards, dtype=jnp.int32)).reshape(TOKENS, Q_HEADS * HD)
    projected_all = jnp.dot(attention, out_weight, preferred_element_type=jnp.float32)
    attended = (residual.astype(jnp.float32) + projected_all).astype(jnp.bfloat16)
    widened = attended.astype(jnp.float32)
    inverse = lax.rsqrt(lax.optimization_barrier(jnp.mean(widened * widened, axis=-1, keepdims=True)) + 1e-06)
    normed = (widened * inverse * norm_gain).astype(jnp.bfloat16)
    entries = TOKENS * TOP
    limit = TOKENS // TOK_LOC * CAP
    flat_experts = routes.reshape(entries)
    flat_weights = route_weights.reshape(entries)
    owners = (jnp.arange(entries, dtype=jnp.int32) // TOP).astype(jnp.int32)

    def add_expert(expert, totals):
        expert = jnp.asarray(expert).astype(jnp.int32)
        chosen = flat_experts == expert
        places = jnp.cumsum(chosen.astype(jnp.int32), dtype=jnp.int32) - 1
        target = jnp.where(chosen, places, limit).astype(jnp.int32)
        picked = jnp.zeros((limit + 1,), jnp.int32).at[target].set(owners)[:limit]
        scales = jnp.zeros((limit + 1,), jnp.float32).at[target].set(flat_weights)[:limit]
        gate_up = lax.dynamic_index_in_dim(expert_gate_up, expert, 0, keepdims=False)
        down_matrix = lax.dynamic_index_in_dim(expert_down, expert, 0, keepdims=False)
        projected = jnp.dot(normed[picked], gate_up, preferred_element_type=jnp.float32)
        hidden = (jax.nn.silu(projected[:, :FFE]) * projected[:, FFE:]).astype(jnp.bfloat16)
        output = jnp.dot(hidden, down_matrix, preferred_element_type=jnp.float32)
        return totals.at[picked].add(scales[:, None] * rounded(output))
    totals = lax.fori_loop(0, EXPERTS, add_expert, jnp.zeros((TOKENS, D), jnp.float32))
    return (attended, totals.astype(jnp.bfloat16))
```

```python
import functools
import math

import jax
import jax.numpy as jnp
from jax import lax
from jax.experimental import pallas as pl
from jax.experimental.pallas import tpu as pltpu
from jax.sharding import PartitionSpec as P

HD = 128
FFE = 768
TOP = 8
BLK = 128
DIST = 3
CAP = 16
CHUNKS = 2
ALL = ("ctx", "head")
BF16 = jnp.bfloat16
F32 = jnp.float32
NT = (((1,), (1,)), ((), ()))
TN = (((0,), (0,)), ((), ()))
EXPONENT = math.log2(math.e) / math.sqrt(HD)
VMEM_LIMIT = 56 * 1024 * 1024


def params(steps=1):
    return pltpu.CompilerParams(
        dimension_semantics=("arbitrary",) * steps, vmem_limit_bytes=VMEM_LIMIT
    )


def attention_kernel(usable, q_ref, k_ref, v_ref, fk_ref, fv_ref, w_ref, out_ref, mixed_ref):
    block = pl.program_id(0)
    heads = q_ref.shape[1] // HD
    blocks = k_ref.shape[0] // BLK

    def attend(at):
        near = at * BLK
        wide = near + BLK
        keys = jnp.concatenate([k_ref[:wide]] + [fk_ref[j] for j in range(DIST)], axis=0)
        values = jnp.concatenate([v_ref[:wide]] + [fv_ref[j] for j in range(DIST)], axis=0)
        rows = lax.broadcasted_iota(jnp.int32, (BLK, BLK), 0)
        columns = lax.broadcasted_iota(jnp.int32, (BLK, BLK), 1)
        parts = [jnp.zeros((BLK, near), F32)] if at else []
        parts.append(jnp.where(rows >= columns, 0.0, -jnp.inf))
        for j in range(DIST):
            parts.append(jnp.full((BLK, BLK), jnp.where(usable[j] > 0, 0.0, -jnp.inf), F32))
        bias = jnp.concatenate(parts, axis=1)
        for n in range(heads):
            query = q_ref[:, n * HD : (n + 1) * HD]
            score = lax.dot_general(query, keys, NT, preferred_element_type=F32) + bias
            highest = jnp.max(score, axis=1, keepdims=True)
            weight = jnp.exp2((score - highest) * EXPONENT)
            denominator = jnp.sum(weight, axis=1, keepdims=True)
            mixed = jnp.dot(weight.astype(BF16), values, preferred_element_type=F32)
            mixed_ref[:, n * HD : (n + 1) * HD] = (mixed / denominator).astype(BF16)

    for at in range(blocks):
        pl.when(block == at)(functools.partial(attend, at))
    out_ref[...] = jnp.dot(mixed_ref[...], w_ref[...], preferred_element_type=F32).astype(BF16)


def attention(usable, queries, keys, values, far_keys, far_values, out_weight):
    length, wide = queries.shape
    width = out_weight.shape[1]
    whole = lambda shape: pl.BlockSpec(
        shape, lambda b, u: (0,) * len(shape), pipeline_mode=pl.Buffered(1)
    )
    return pl.pallas_call(
        attention_kernel,
        grid_spec=pltpu.PrefetchScalarGridSpec(
            num_scalar_prefetch=1,
            grid=(length // BLK,),
            in_specs=[
                pl.BlockSpec((BLK, wide), lambda b, u: (b, 0)),
                whole(keys.shape),
                whole(values.shape),
                pl.BlockSpec((DIST, BLK, HD), lambda b, u: (0, b, 0)),
                pl.BlockSpec((DIST, BLK, HD), lambda b, u: (0, b, 0)),
                whole(out_weight.shape),
            ],
            out_specs=pl.BlockSpec((BLK, width), lambda b, u: (b, 0)),
            scratch_shapes=[pltpu.VMEM((BLK, wide), BF16)],
        ),
        out_shape=jax.ShapeDtypeStruct((length, width), BF16),
        compiler_params=params(),
        name="attention",
    )(usable, queries, keys, values, far_keys, far_values, out_weight)


def tables_kernel(routes_ref, weights_ref, send_ref, high_ref, low_ref):
    top, tokens = routes_ref.shape
    experts = send_ref.shape[1]
    chunks, slots = send_ref.shape[0], send_ref.shape[2]
    names = lax.broadcasted_iota(jnp.int32, (experts, tokens), 0)
    chosen = jnp.zeros((experts, tokens), F32)
    weight = jnp.zeros((experts, tokens), F32)
    for k in range(top):
        here = routes_ref[k : k + 1, :] == names
        chosen = jnp.where(here, 1.0, chosen)
        weight = jnp.where(here, weights_ref[k : k + 1, :], weight)
    before = (
        lax.broadcasted_iota(jnp.int32, (tokens, tokens), 0)
        < lax.broadcasted_iota(jnp.int32, (tokens, tokens), 1)
    ).astype(BF16)
    place = jnp.dot(chosen.astype(BF16), before, preferred_element_type=F32)
    place = jnp.where(chosen > 0.0, place, -1.0)
    high = weight.astype(BF16).astype(F32)
    low = weight - high
    for c in range(chunks):
        for s in range(slots):
            here = place == float(c * slots + s)
            send_ref[c, :, s, :] = jnp.where(here, 1.0, 0.0)
            high_ref[c, :, s, :] = jnp.where(here, high, 0.0)
            low_ref[c, :, s, :] = jnp.where(here, low, 0.0)


def tables(routes, route_weights, experts):
    tokens = routes.shape[0]
    shape = jax.ShapeDtypeStruct((CHUNKS, experts, CAP // CHUNKS, tokens), F32)
    send, high, low = pl.pallas_call(
        tables_kernel, out_shape=(shape,) * 3, compiler_params=params(0), name="tables"
    )(routes.T, route_weights.T)
    rows = experts * CAP // CHUNKS
    flat = lambda a: a.reshape(CHUNKS, rows, tokens).astype(BF16)
    return flat(send), jnp.concatenate([flat(high), flat(low)], axis=2)


def norm_kernel(parts_ref, residual_ref, gain_ref, send_ref, attended_ref, normed_ref, out_ref):
    @pl.when(pl.program_id(0) == 0)
    def _():
        total = residual_ref[...].astype(F32)
        for i in range(parts_ref.shape[0]):
            total = total + parts_ref[i].astype(F32)
        attended = total.astype(BF16)
        attended_ref[...] = attended
        wide = attended.astype(F32)
        inverse = lax.rsqrt(jnp.mean(wide * wide, axis=1, keepdims=True) + 1e-06)
        normed_ref[...] = (wide * inverse * gain_ref[...]).astype(BF16)

    out_ref[...] = jnp.dot(send_ref[...], normed_ref[...], preferred_element_type=F32).astype(BF16)


def norm_dispatch(parts, residual, gain, send):
    tokens, width = residual.shape
    rows = send.shape[0]
    step = 256
    whole = lambda shape: pl.BlockSpec(shape, lambda i: (0,) * len(shape))
    return pl.pallas_call(
        norm_kernel,
        grid=(rows // step,),
        in_specs=[
            whole(parts.shape),
            whole(residual.shape),
            whole((1, width)),
            pl.BlockSpec((step, tokens), lambda i: (i, 0)),
        ],
        out_specs=(
            whole((tokens, width)),
            whole((tokens, width)),
            pl.BlockSpec((step, width), lambda i: (i, 0)),
        ),
        out_shape=(
            jax.ShapeDtypeStruct((tokens, width), BF16),
            jax.ShapeDtypeStruct((tokens, width), BF16),
            jax.ShapeDtypeStruct((rows, width), BF16),
        ),
        compiler_params=params(),
        name="norm_dispatch",
    )(parts, residual, gain.reshape(1, width), send)


def dispatch_kernel(send_ref, normed_ref, out_ref):
    out_ref[...] = jnp.dot(send_ref[...], normed_ref[...], preferred_element_type=F32).astype(BF16)


def dispatch(send, normed):
    tokens, width = normed.shape
    rows = send.shape[0]
    step = 256
    return pl.pallas_call(
        dispatch_kernel,
        grid=(rows // step,),
        in_specs=[
            pl.BlockSpec((step, tokens), lambda i: (i, 0)),
            pl.BlockSpec((tokens, width), lambda i: (0, 0)),
        ],
        out_specs=pl.BlockSpec((step, width), lambda i: (i, 0)),
        out_shape=jax.ShapeDtypeStruct((rows, width), BF16),
        compiler_params=params(),
        name="dispatch",
    )(send, normed)


def expert_kernel(x_ref, gate_up_ref, down_ref, out_ref):
    projected = jnp.dot(x_ref[...], gate_up_ref[0], preferred_element_type=F32)
    gate, up = projected[:, :FFE], projected[:, FFE:]
    hidden = (gate / (1.0 + jnp.exp(-gate)) * up).astype(BF16)
    out_ref[...] = jnp.dot(hidden, down_ref[0], preferred_element_type=F32).astype(BF16)


def expert(x, gate_up, down):
    rows, width = x.shape
    step = 256
    whole = lambda shape: pl.BlockSpec(
        shape, lambda i: (0,) * len(shape), pipeline_mode=pl.Buffered(1)
    )
    return pl.pallas_call(
        expert_kernel,
        grid=(rows // step,),
        in_specs=[
            pl.BlockSpec((step, width), lambda i: (i, 0)),
            whole(gate_up.shape),
            whole(down.shape),
        ],
        out_specs=pl.BlockSpec((step, width), lambda i: (i, 0)),
        out_shape=jax.ShapeDtypeStruct((rows, width), BF16),
        compiler_params=params(),
        name="expert",
    )(x, gate_up, down)


def combine_kernel(table_ref, rows_ref, *refs):
    before_ref, (out_ref, total_ref) = (refs[0] if len(refs) == 3 else None), refs[-2:]
    step = pl.program_id(0)
    tokens = out_ref.shape[0]
    part = lax.dot_general(table_ref[...], rows_ref[...], TN, preferred_element_type=F32)
    part = part[:tokens] + part[tokens:]

    @pl.when(step == 0)
    def _():
        total_ref[...] = part if before_ref is None else part + before_ref[...]

    @pl.when(step > 0)
    def _():
        total_ref[...] += part

    @pl.when(step == pl.num_programs(0) - 1)
    def _():
        out_ref[...] = total_ref[...].astype(out_ref.dtype)


def combine(table, rows, before, dtype):
    count, width = rows.shape
    tokens = table.shape[1] // 2
    step = 256
    whole = lambda shape: pl.BlockSpec(shape, lambda i: (0,) * len(shape))
    operands = (table, rows) + (() if before is None else (before,))
    return pl.pallas_call(
        combine_kernel,
        grid=(count // step,),
        in_specs=[
            pl.BlockSpec((step, 2 * tokens), lambda i: (i, 0)),
            pl.BlockSpec((step, width), lambda i: (i, 0)),
        ]
        + ([] if before is None else [whole(before.shape)]),
        out_specs=whole((tokens, width)),
        out_shape=jax.ShapeDtypeStruct((tokens, width), dtype),
        scratch_shapes=[pltpu.VMEM((tokens, width), F32)],
        compiler_params=params(),
        name="combine",
    )(*operands)


def body(
    queries,
    keys,
    values,
    distances,
    out_weight,
    residual,
    norm_gain,
    expert_gate_up,
    expert_down,
    routes,
    route_weights,
):
    length = queries.shape[0]
    tokens, width = residual.shape
    devices = lax.axis_size(ALL)
    group = lax.axis_size("head")
    source = lax.axis_index("ctx") - distances[0]
    usable = (source >= 0).astype(jnp.int32)
    packed = jnp.concatenate([keys, values], axis=1)
    everything = lax.all_gather(packed, "ctx", axis=0, tiled=True)
    offsets = jnp.maximum(source, 0) * length
    fetched = jnp.stack(
        [lax.dynamic_slice_in_dim(everything, offsets[j], length, 0) for j in range(DIST)]
    )
    far_keys, far_values = fetched[:, :, :HD], fetched[:, :, HD:]
    projected = attention(usable, queries, keys, values, far_keys, far_values, out_weight)
    parts = lax.all_to_all(projected, "head", split_axis=0, concat_axis=0, tiled=True)
    send, table = tables(routes, route_weights, devices)
    attended, normed, first = norm_dispatch(
        parts.reshape(group, tokens, width), residual, norm_gain, send[0]
    )
    exchange = lambda a: lax.all_to_all(a, ALL, split_axis=0, concat_axis=0, tiled=True)
    arrived = [exchange(first)]
    for c in range(1, CHUNKS):
        arrived.append(exchange(dispatch(send[c], normed)))
    returned = [exchange(expert(a, expert_gate_up, expert_down)) for a in arrived]
    total = None
    for c in range(CHUNKS):
        total = combine(table[c], returned[c], total, BF16 if c == CHUNKS - 1 else F32)
    return (attended, total)


def solution(mesh):
    return jax.shard_map(
        body,
        mesh=mesh,
        in_specs=(
            P("ctx", "head"),
            P("ctx", "head"),
            P("ctx", "head"),
            P("head", None),
            P("head", None),
            P(ALL, None),
            P(),
            P(ALL, None, None),
            P(ALL, None, None),
            P(ALL, None),
            P(ALL, None),
        ),
        out_specs=(P(ALL, None), P(ALL, None)),
        check_vma=False,
    )
```

```python
import functools
import math

import jax
import jax.numpy as jnp
from jax import lax
from jax.experimental import pallas as pl
from jax.experimental.pallas import tpu as pltpu
from jax.sharding import PartitionSpec as P

HD = 128
FFE = 768
TOP = 8
BLK = 128
DIST = 3
CAP = 16
CHUNKS = 2
ALL = ("ctx", "head")
BF16 = jnp.bfloat16
F32 = jnp.float32
NT = (((1,), (1,)), ((), ()))
TN = (((0,), (0,)), ((), ()))
EXPONENT = math.log2(math.e) / math.sqrt(HD)
VMEM_LIMIT = 56 * 1024 * 1024


def params(steps=1):
    return pltpu.CompilerParams(
        dimension_semantics=("arbitrary",) * steps, vmem_limit_bytes=VMEM_LIMIT
    )


def near_kernel(q_ref, k_ref, v_ref, mixed_ref, stats_ref):
    block = pl.program_id(0)
    heads = q_ref.shape[1] // HD
    blocks = k_ref.shape[0] // BLK

    def attend(at):
        near = at * BLK
        keys, values = k_ref[: near + BLK], v_ref[: near + BLK]
        rows = lax.broadcasted_iota(jnp.int32, (BLK, BLK), 0)
        columns = lax.broadcasted_iota(jnp.int32, (BLK, BLK), 1)
        bias = jnp.where(rows >= columns, 0.0, -jnp.inf)
        if at:
            bias = jnp.concatenate([jnp.zeros((BLK, near), F32), bias], axis=1)
        stats = jnp.zeros((BLK, HD), F32)
        for n in range(heads):
            query = q_ref[:, n * HD : (n + 1) * HD]
            score = lax.dot_general(query, keys, NT, preferred_element_type=F32) + bias
            highest = jnp.max(score, axis=1, keepdims=True)
            weight = jnp.exp2((score - highest) * EXPONENT)
            stats = jnp.where(columns == n, highest, stats)
            stats = jnp.where(
                columns == heads + n, jnp.sum(weight, axis=1, keepdims=True), stats
            )
            mixed_ref[:, n * HD : (n + 1) * HD] = jnp.dot(
                weight.astype(BF16), values, preferred_element_type=F32
            )
        stats_ref[...] = stats

    for at in range(blocks):
        pl.when(block == at)(functools.partial(attend, at))


def near_attention(queries, keys, values):
    length, wide = queries.shape
    whole = lambda shape: pl.BlockSpec(shape, lambda b: (0,) * len(shape))
    rows = lambda columns: pl.BlockSpec((BLK, columns), lambda b: (b, 0))
    return pl.pallas_call(
        near_kernel,
        grid=(length // BLK,),
        in_specs=[rows(wide), whole(keys.shape), whole(values.shape)],
        out_specs=(rows(wide), rows(HD)),
        out_shape=(
            jax.ShapeDtypeStruct((length, wide), F32),
            jax.ShapeDtypeStruct((length, HD), F32),
        ),
        compiler_params=params(),
        name="near_attention",
    )(queries, keys, values)


def far_kernel(
    place, wanted, q_ref, mine_ref, other_ref, near_ref, stats_ref, w_ref, out_ref, mixed_ref
):
    heads = q_ref.shape[1] // HD
    keys, values, bias = [], [], []
    for j in range(DIST):
        swapped = lax.rem(wanted[0, j], 2) > 0
        keys.append(jnp.where(swapped, other_ref[0, j], mine_ref[0, j]))
        values.append(jnp.where(swapped, other_ref[1, j], mine_ref[1, j]))
        reach = jnp.where(place[1] >= wanted[0, j], 0.0, -jnp.inf)
        bias.append(jnp.full((BLK, BLK), reach, F32))
    keys, values = jnp.concatenate(keys, axis=0), jnp.concatenate(values, axis=0)
    bias = jnp.concatenate(bias, axis=1)
    for n in range(heads):
        span = slice(n * HD, (n + 1) * HD)
        score = lax.dot_general(q_ref[:, span], keys, NT, preferred_element_type=F32) + bias
        before = stats_ref[:, n : n + 1]
        highest = jnp.maximum(jnp.max(score, axis=1, keepdims=True), before)
        weight = jnp.exp2((score - highest) * EXPONENT)
        keep = jnp.exp2((before - highest) * EXPONENT)
        denominator = jnp.sum(weight, axis=1, keepdims=True)
        denominator = denominator + keep * stats_ref[:, heads + n : heads + n + 1]
        mixed = jnp.dot(weight.astype(BF16), values, preferred_element_type=F32)
        mixed = mixed + keep * near_ref[:, span]
        mixed_ref[:, span] = (mixed / denominator).astype(BF16)
    out_ref[...] = jnp.dot(mixed_ref[...], w_ref[...], preferred_element_type=F32).astype(BF16)


def far_attention(place, wanted, queries, mine, other, near, stats, out_weight, count):
    wide, width = queries.shape[1], out_weight.shape[1]
    blocks = queries.shape[0] // BLK
    at = lambda i, place: lax.rem(place[0] + i, blocks)
    rows = lambda columns: pl.BlockSpec((BLK, columns), lambda i, p, w: (at(i, p), 0))
    far = pl.BlockSpec((2, DIST, BLK, HD), lambda i, p, w: (0, 0, at(i, p), 0))
    return pl.pallas_call(
        far_kernel,
        grid_spec=pltpu.PrefetchScalarGridSpec(
            num_scalar_prefetch=2,
            grid=(count,),
            in_specs=[
                rows(wide),
                far,
                far,
                rows(wide),
                rows(HD),
                pl.BlockSpec(
                    out_weight.shape, lambda i, p, w: (0, 0), pipeline_mode=pl.Buffered(1)
                ),
            ],
            out_specs=pl.BlockSpec((BLK, width), lambda i, p, w: (i, 0)),
            scratch_shapes=[pltpu.VMEM((BLK, wide), BF16)],
        ),
        out_shape=jax.ShapeDtypeStruct((count * BLK, width), BF16),
        compiler_params=params(),
        name="far_attention",
    )(place, wanted, queries, mine, other, near, stats, out_weight)


def pick_kernel(place, wanted, *refs):
    key_refs, value_refs, out_ref, sems = refs[:5], refs[5:10], refs[10], refs[11]
    me = place[0]
    core = lax.rem(me, 2)
    for j in range(DIST):
        asked = me - core + lax.rem(core + wanted[0, j], 2)
        source = asked - wanted[0, j]
        source = jnp.where(source >= 0, source, me)
        over_z = lax.rem(me // 8 - source // 8 + 4, 4)
        over_x = lax.rem(lax.rem(me // 2, 4) - lax.rem(source // 2, 4) + 4, 4)
        for kind, pieces, outer, inner in (
            (0, key_refs, over_x, over_z),
            (1, value_refs, over_z, over_x),
        ):
            target, sem = out_ref.at[kind, j], sems.at[kind, j]

            def fetch(piece, row, target=target, sem=sem):
                pltpu.make_async_copy(piece.at[row], target, sem).start()

            for step in (0, 1, 3):
                pl.when(outer == step)(functools.partial(fetch, pieces[step], inner))
            pl.when((outer == 2) & (inner < 2))(functools.partial(fetch, pieces[2], inner))
            pl.when((outer == 2) & (inner >= 2))(functools.partial(fetch, pieces[4], inner - 2))
    for j in range(DIST):
        for kind, pieces in ((0, key_refs), (1, value_refs)):
            pltpu.make_async_copy(
                pieces[0].at[0], out_ref.at[kind, j], sems.at[kind, j]
            ).wait()


def pick(place, wanted, key_pieces, value_pieces):
    anywhere = pl.BlockSpec(memory_space=pl.ANY)
    length = key_pieces[0].shape[1]
    return pl.pallas_call(
        pick_kernel,
        grid_spec=pltpu.PrefetchScalarGridSpec(
            num_scalar_prefetch=2,
            grid=(1,),
            in_specs=[anywhere] * 10,
            out_specs=anywhere,
            scratch_shapes=[pltpu.SemaphoreType.DMA((2, DIST))],
        ),
        out_shape=jax.ShapeDtypeStruct((2, DIST, length, HD), BF16),
        compiler_params=params(),
        name="pick",
    )(place, wanted, *key_pieces, *value_pieces)


def moves(side):
    def along_z(step):
        return [(i, (i + 8 * step) % 32) for i in range(32)]

    def along_x(step):
        return [(i, i - i % 8 + (i + 2 * step) % 8) for i in range(32)]

    return (along_z if side == "z" else along_x)(1), (along_z if side == "z" else along_x)(-1)


def circle(block, side, axis):
    forward, backward = moves(side)
    send = lambda a, pairs: lax.ppermute(a, "ctx", pairs)
    half = block.shape[axis] // 2
    low = lambda a: lax.slice_in_dim(a, 0, half, axis=axis)
    high = lambda a: lax.slice_in_dim(a, half, 2 * half, axis=axis)
    one, three = send(block, forward), send(block, backward)
    return one, send(low(one), forward), three, send(high(three), backward)


def tables_kernel(routes_ref, weights_ref, send_ref, table_ref, spread_ref):
    top, tokens = routes_ref.shape
    experts, slots = spread_ref.shape[:2]
    chunks = send_ref.shape[0]
    names = lax.broadcasted_iota(jnp.int32, (experts, tokens), 0)
    chosen = jnp.zeros((experts, tokens), F32)
    weight = jnp.zeros((experts, tokens), F32)
    for k in range(top):
        here = routes_ref[k : k + 1, :] == names
        chosen = jnp.where(here, 1.0, chosen)
        weight = jnp.where(here, weights_ref[k : k + 1, :], weight)
    before = (
        lax.broadcasted_iota(jnp.int32, (tokens, tokens), 0)
        < lax.broadcasted_iota(jnp.int32, (tokens, tokens), 1)
    ).astype(BF16)
    place = jnp.dot(chosen.astype(BF16), before, preferred_element_type=F32)
    place = jnp.where(chosen > 0.0, place, -1.0)
    high = weight.astype(BF16).astype(F32)
    low = weight - high

    def spread(c, value):
        for s in range(slots):
            spread_ref[:, s, :] = jnp.where(place == float(c * slots + s), value, 0.0)
        return spread_ref[...].reshape(experts * slots, tokens).astype(BF16)

    for c in range(chunks):
        send_ref[c] = spread(c, 1.0)
        table_ref[c, :, :tokens] = spread(c, high)
        table_ref[c, :, tokens:] = spread(c, low)


def tables(routes, route_weights, experts):
    tokens = routes.shape[0]
    slots = CAP // CHUNKS
    return pl.pallas_call(
        tables_kernel,
        out_shape=(
            jax.ShapeDtypeStruct((CHUNKS, experts * slots, tokens), BF16),
            jax.ShapeDtypeStruct((CHUNKS, experts * slots, 2 * tokens), BF16),
        ),
        scratch_shapes=[pltpu.VMEM((experts, slots, tokens), F32)],
        compiler_params=params(0),
        name="tables",
    )(routes.T, route_weights.T)


def norm_kernel(
    own_ref, left_ref, right_ref, residual_ref, gain_ref, send_ref, attended_ref, normed_ref, out_ref
):
    @pl.when(pl.program_id(0) == 0)
    def _():
        total = residual_ref[...].astype(F32) + own_ref[...].astype(F32)
        total = total + left_ref[...].astype(F32) + right_ref[...].astype(F32)
        attended = total.astype(BF16)
        attended_ref[...] = attended
        wide = attended.astype(F32)
        inverse = lax.rsqrt(jnp.mean(wide * wide, axis=1, keepdims=True) + 1e-06)
        normed_ref[...] = (wide * inverse * gain_ref[...]).astype(BF16)

    out_ref[...] = jnp.dot(send_ref[0], normed_ref[...], preferred_element_type=F32).astype(BF16)


def norm_dispatch(own, left, right, residual, gain, send):
    tokens, width = residual.shape
    rows = send.shape[1]
    step = 256
    whole = lambda shape: pl.BlockSpec(shape, lambda i: (0,) * len(shape))
    return pl.pallas_call(
        norm_kernel,
        grid=(rows // step,),
        in_specs=[whole((tokens, width))] * 4
        + [whole((1, width)), pl.BlockSpec((1, step, tokens), lambda i: (0, i, 0))],
        out_specs=(
            whole((tokens, width)),
            whole((tokens, width)),
            pl.BlockSpec((step, width), lambda i: (i, 0)),
        ),
        out_shape=(
            jax.ShapeDtypeStruct((tokens, width), BF16),
            jax.ShapeDtypeStruct((tokens, width), BF16),
            jax.ShapeDtypeStruct((rows, width), BF16),
        ),
        compiler_params=params(),
        name="norm_dispatch",
    )(own, left, right, residual, gain.reshape(1, width), send)


def dispatch_kernel(send_ref, normed_ref, out_ref):
    out_ref[...] = jnp.dot(send_ref[0], normed_ref[...], preferred_element_type=F32).astype(BF16)


def dispatch(send, normed, chunk):
    tokens, width = normed.shape
    rows = send.shape[1]
    step = 256
    return pl.pallas_call(
        dispatch_kernel,
        grid=(rows // step,),
        in_specs=[
            pl.BlockSpec((1, step, tokens), lambda i: (chunk, i, 0)),
            pl.BlockSpec((tokens, width), lambda i: (0, 0)),
        ],
        out_specs=pl.BlockSpec((step, width), lambda i: (i, 0)),
        out_shape=jax.ShapeDtypeStruct((rows, width), BF16),
        compiler_params=params(),
        name="dispatch",
    )(send, normed)


def expert_kernel(x_ref, gate_up_ref, down_ref, out_ref):
    projected = jnp.dot(x_ref[...], gate_up_ref[0], preferred_element_type=F32)
    gate, up = projected[:, :FFE], projected[:, FFE:]
    hidden = (gate / (1.0 + jnp.exp(-gate)) * up).astype(BF16)
    out_ref[...] = jnp.dot(hidden, down_ref[0], preferred_element_type=F32).astype(BF16)


def expert(x, gate_up, down):
    rows, width = x.shape
    step = 256
    whole = lambda shape: pl.BlockSpec(
        shape, lambda i: (0,) * len(shape), pipeline_mode=pl.Buffered(1)
    )
    return pl.pallas_call(
        expert_kernel,
        grid=(rows // step,),
        in_specs=[
            pl.BlockSpec((step, width), lambda i: (i, 0)),
            whole(gate_up.shape),
            whole(down.shape),
        ],
        out_specs=pl.BlockSpec((step, width), lambda i: (i, 0)),
        out_shape=jax.ShapeDtypeStruct((rows, width), BF16),
        compiler_params=params(),
        name="expert",
    )(x, gate_up, down)


def combine_kernel(table_ref, rows_ref, *refs):
    before_ref, (out_ref, total_ref) = (refs[0] if len(refs) == 3 else None), refs[-2:]
    step = pl.program_id(0)
    tokens = out_ref.shape[0]
    part = lax.dot_general(table_ref[0], rows_ref[...], TN, preferred_element_type=F32)
    part = part[:tokens] + part[tokens:]

    @pl.when(step == 0)
    def _():
        total_ref[...] = part if before_ref is None else part + before_ref[...]

    @pl.when(step > 0)
    def _():
        total_ref[...] += part

    @pl.when(step == pl.num_programs(0) - 1)
    def _():
        out_ref[...] = total_ref[...].astype(out_ref.dtype)


def combine(table, rows, before, dtype, chunk):
    count, width = rows.shape
    tokens = table.shape[2] // 2
    step = 256
    whole = lambda shape: pl.BlockSpec(shape, lambda i: (0,) * len(shape))
    operands = (table, rows) + (() if before is None else (before,))
    return pl.pallas_call(
        combine_kernel,
        grid=(count // step,),
        in_specs=[
            pl.BlockSpec((1, step, 2 * tokens), lambda i: (chunk, i, 0)),
            pl.BlockSpec((step, width), lambda i: (i, 0)),
        ]
        + ([] if before is None else [whole(before.shape)]),
        out_specs=whole((tokens, width)),
        out_shape=jax.ShapeDtypeStruct((tokens, width), dtype),
        scratch_shapes=[pltpu.VMEM((tokens, width), F32)],
        compiler_params=params(),
        name="combine",
    )(*operands)


def body(
    queries,
    keys,
    values,
    distances,
    out_weight,
    residual,
    norm_gain,
    expert_gate_up,
    expert_down,
    routes,
    route_weights,
):
    tokens, width = residual.shape
    devices = lax.axis_size(ALL)
    me, head = lax.axis_index("ctx"), lax.axis_index("head")
    k1, k2a, k3, k2b = circle(keys, "z", 0)
    v1, v2a, v3, v2b = circle(values, "x", 0)
    key_line = jnp.stack([keys, k1, jnp.concatenate([k2a, k2b], axis=0), k3])
    value_line = jnp.stack([values, v1, jnp.concatenate([v2a, v2b], axis=0), v3])
    key_pieces = (key_line,) + circle(key_line, "x", 0)
    value_pieces = (value_line,) + circle(value_line, "z", 0)
    near, stats = near_attention(queries, keys, values)
    send, table = tables(routes, route_weights, devices)
    mine = pick(me.reshape(1), distances, key_pieces, value_pieces)
    other = lax.ppermute(mine, "ctx", [(i, i ^ 1) for i in range(32)])

    def project(first, count):
        place = jnp.stack([lax.rem(head + first, 4), me])
        return far_attention(
            place, distances, queries, mine, other, near, stats, out_weight, count
        )

    up = [(i, (i + 1) % 4) for i in range(4)]
    down = [(i, (i + 3) % 4) for i in range(4)]
    over_head = lambda a, pairs: lax.ppermute(a, "head", pairs)
    half = width // 2
    across = project(2, 1)
    from_left = over_head(across[:, :half], up)
    from_right = over_head(across[:, half:], down)
    after = project(1, 1)
    before = project(3, 1)
    add = lambda a, b: (a.astype(F32) + b.astype(F32)).astype(BF16)
    after = jnp.concatenate([add(after[:, :half], from_left), after[:, half:]], axis=1)
    before = jnp.concatenate([before[:, :half], add(before[:, half:], from_right)], axis=1)
    left, right = over_head(after, up), over_head(before, down)
    own = project(0, 1)
    attended, normed, first = norm_dispatch(own, left, right, residual, norm_gain, send)
    exchange = lambda a: lax.all_to_all(a, ALL, split_axis=0, concat_axis=0, tiled=True)
    arrived = [exchange(first)]
    for c in range(1, CHUNKS):
        arrived.append(exchange(dispatch(send, normed, c)))
    returned = [exchange(expert(a, expert_gate_up, expert_down)) for a in arrived]
    total = None
    for c in range(CHUNKS):
        total = combine(table, returned[c], total, BF16 if c == CHUNKS - 1 else F32, c)
    return (attended, total)


def solution(mesh):
    return jax.shard_map(
        body,
        mesh=mesh,
        in_specs=(
            P("ctx", "head"),
            P("ctx", "head"),
            P("ctx", "head"),
            P("head", None),
            P("head", None),
            P(ALL, None),
            P(),
            P(ALL, None, None),
            P(ALL, None, None),
            P(ALL, None),
            P(ALL, None),
        ),
        out_specs=(P(ALL, None), P(ALL, None)),
        check_vma=False,
    )
```

```python
import functools
import math

import jax
import jax.numpy as jnp
from jax import lax
from jax.experimental import pallas as pl
from jax.experimental.pallas import tpu as pltpu
from jax.sharding import PartitionSpec as P

HD = 128
FFE = 768
TOP = 8
BLK = 128
DIST = 3
CAP = 16
CHUNKS = 2
PAIR = 2
ALL = ("ctx", "head")
BF16 = jnp.bfloat16
F32 = jnp.float32
NT = (((1,), (1,)), ((), ()))
TN = (((0,), (0,)), ((), ()))
EXPONENT = math.log2(math.e) / math.sqrt(HD)
VMEM_LIMIT = 56 * 1024 * 1024


def params(steps=1):
    return pltpu.CompilerParams(
        dimension_semantics=("arbitrary",) * steps, vmem_limit_bytes=VMEM_LIMIT
    )


def attention_kernel(
    place, wanted, q_ref, k_ref, v_ref, far0_ref, far1_ref, far2_ref, w_ref, *refs
):
    out_refs, mixed_ref = refs[:-1], refs[-1]
    step = pl.program_id(0)
    blocks = k_ref.shape[0] // BLK
    heads = q_ref.shape[1] // HD
    block = lax.rem(place[0] + step, blocks)
    far_refs = (far0_ref, far1_ref, far2_ref)

    def attend(at):
        near = at * BLK
        later = lax.broadcasted_iota(jnp.int32, (BLK, BLK), 0) > lax.broadcasted_iota(
            jnp.int32, (BLK, BLK), 1
        )
        bias = jnp.where(later, -jnp.inf, 0.0)
        bias = jnp.concatenate([bias] * PAIR, axis=1)
        reach = [jnp.where(place[1] >= wanted[0, j], 0.0, -jnp.inf) for j in range(DIST)]
        keys = jnp.concatenate([k_ref[: near + BLK]] + [r[0] for r in far_refs], axis=0)
        values = jnp.concatenate([v_ref[: near + BLK]] + [r[1] for r in far_refs], axis=0)
        for n in range(0, heads, PAIR):
            query = jnp.concatenate(
                [q_ref[:, (n + i) * HD : (n + i + 1) * HD] for i in range(PAIR)], axis=0
            )
            score = lax.dot_general(keys, query, NT, preferred_element_type=F32)
            parts = [score[:near]] if at else []
            parts.append(score[near : near + BLK] + bias)
            for j in range(DIST):
                start = near + (j + 1) * BLK
                parts.append(score[start : start + BLK] + reach[j])
            score = jnp.concatenate(parts, axis=0)
            highest = jnp.max(score, axis=0, keepdims=True)
            weight = jnp.exp2((score - highest) * EXPONENT)
            denominator = jnp.sum(weight, axis=0, keepdims=True)
            mixed = lax.dot_general(values, weight.astype(BF16), TN, preferred_element_type=F32)
            mixed = mixed / denominator
            for i in range(PAIR):
                mixed_ref[pl.ds(step * BLK, BLK), (n + i) * HD : (n + i + 1) * HD] = (
                    mixed[:, i * BLK : (i + 1) * BLK].T.astype(BF16)
                )

    for at in range(blocks):
        pl.when(block == at)(functools.partial(attend, at))

    @pl.when(step == blocks - 1)
    def _():
        for i, out_ref in enumerate(out_refs):
            out_ref[...] = jnp.dot(
                mixed_ref[i * BLK : (i + 1) * BLK], w_ref[...], preferred_element_type=F32
            ).astype(BF16)


def attention(place, wanted, queries, keys, values, far, out_weight):
    length, wide = queries.shape
    width = out_weight.shape[1]
    blocks = length // BLK
    at = lambda i, place: lax.rem(place[0] + i, blocks)
    whole = lambda shape: pl.BlockSpec(
        shape, lambda i, p, w: (0,) * len(shape), pipeline_mode=pl.Buffered(1)
    )
    return pl.pallas_call(
        attention_kernel,
        grid_spec=pltpu.PrefetchScalarGridSpec(
            num_scalar_prefetch=2,
            grid=(blocks,),
            in_specs=[
                pl.BlockSpec((BLK, wide), lambda i, p, w: (at(i, p), 0)),
                whole(keys.shape),
                whole(values.shape),
            ]
            + [pl.BlockSpec((2, BLK, HD), lambda i, p, w: (0, at(i, p), 0))] * DIST
            + [whole(out_weight.shape)],
            out_specs=(whole((BLK, width)),) * blocks,
            scratch_shapes=[pltpu.VMEM((length, wide), BF16)],
        ),
        out_shape=(jax.ShapeDtypeStruct((BLK, width), BF16),) * blocks,
        compiler_params=params(),
        name="attention",
    )(place, wanted, queries, keys, values, *far, out_weight)


def tables_kernel(routes_ref, weights_ref, send_ref, table_ref, spread_ref):
    top, tokens = routes_ref.shape
    experts, slots = spread_ref.shape[:2]
    chunks = send_ref.shape[0]
    names = lax.broadcasted_iota(jnp.int32, (experts, tokens), 0)
    chosen = jnp.zeros((experts, tokens), F32)
    weight = jnp.zeros((experts, tokens), F32)
    for k in range(top):
        here = routes_ref[k : k + 1, :] == names
        chosen = jnp.where(here, 1.0, chosen)
        weight = jnp.where(here, weights_ref[k : k + 1, :], weight)
    before = (
        lax.broadcasted_iota(jnp.int32, (tokens, tokens), 0)
        < lax.broadcasted_iota(jnp.int32, (tokens, tokens), 1)
    ).astype(BF16)
    place = jnp.dot(chosen.astype(BF16), before, preferred_element_type=F32)
    place = jnp.where(chosen > 0.0, place, -1.0)
    high = weight.astype(BF16).astype(F32)
    low = weight - high

    def spread(c, value):
        for s in range(slots):
            spread_ref[:, s, :] = jnp.where(place == float(c * slots + s), value, 0.0)
        return spread_ref[...].reshape(experts * slots, tokens).astype(BF16)

    for c in range(chunks):
        send_ref[c] = spread(c, 1.0)
        table_ref[c, :, :tokens] = spread(c, high)
        table_ref[c, :, tokens:] = spread(c, low)


def tables(routes, route_weights, experts):
    tokens = routes.shape[0]
    slots = CAP // CHUNKS
    return pl.pallas_call(
        tables_kernel,
        out_shape=(
            jax.ShapeDtypeStruct((CHUNKS, experts * slots, tokens), BF16),
            jax.ShapeDtypeStruct((CHUNKS, experts * slots, 2 * tokens), BF16),
        ),
        scratch_shapes=[pltpu.VMEM((experts, slots, tokens), F32)],
        compiler_params=params(0),
        name="tables",
    )(routes.T, route_weights.T)


def norm_kernel(
    own_ref, r1_ref, r2_ref, r3_ref, residual_ref, gain_ref, send_ref, attended_ref, normed_ref, out_ref
):
    @pl.when(pl.program_id(0) == 0)
    def _():
        total = residual_ref[...].astype(F32) + own_ref[...].astype(F32)
        for part_ref in (r1_ref, r2_ref, r3_ref):
            total = total + part_ref[...].astype(F32)
        attended = total.astype(BF16)
        attended_ref[...] = attended
        wide = attended.astype(F32)
        inverse = lax.rsqrt(jnp.mean(wide * wide, axis=1, keepdims=True) + 1e-06)
        normed_ref[...] = (wide * inverse * gain_ref[...]).astype(BF16)

    out_ref[...] = jnp.dot(send_ref[0], normed_ref[...], preferred_element_type=F32).astype(BF16)


def norm_dispatch(own, others, residual, gain, send):
    tokens, width = residual.shape
    rows = send.shape[1]
    step = 256
    whole = lambda shape: pl.BlockSpec(shape, lambda i: (0,) * len(shape))
    return pl.pallas_call(
        norm_kernel,
        grid=(rows // step,),
        in_specs=[pl.BlockSpec(memory_space=pltpu.VMEM)] * 4
        + [whole((tokens, width)), whole((1, width)), pl.BlockSpec((1, step, tokens), lambda i: (0, i, 0))],
        out_specs=(
            whole((tokens, width)),
            whole((tokens, width)),
            pl.BlockSpec((step, width), lambda i: (i, 0)),
        ),
        out_shape=(
            jax.ShapeDtypeStruct((tokens, width), BF16),
            jax.ShapeDtypeStruct((tokens, width), BF16),
            jax.ShapeDtypeStruct((rows, width), BF16),
        ),
        compiler_params=params(),
        name="norm_dispatch",
    )(own, *others, residual, gain.reshape(1, width), send)


def dispatch_kernel(send_ref, normed_ref, out_ref):
    out_ref[...] = jnp.dot(send_ref[0], normed_ref[...], preferred_element_type=F32).astype(BF16)


def dispatch(send, normed, chunk):
    tokens, width = normed.shape
    rows = send.shape[1]
    step = 256
    return pl.pallas_call(
        dispatch_kernel,
        grid=(rows // step,),
        in_specs=[
            pl.BlockSpec((1, step, tokens), lambda i: (chunk, i, 0)),
            pl.BlockSpec((tokens, width), lambda i: (0, 0)),
        ],
        out_specs=pl.BlockSpec((step, width), lambda i: (i, 0)),
        out_shape=jax.ShapeDtypeStruct((rows, width), BF16),
        compiler_params=params(),
        name="dispatch",
    )(send, normed)


def expert_kernel(x_ref, gate_up_ref, down_ref, out_ref):
    projected = jnp.dot(x_ref[...], gate_up_ref[0], preferred_element_type=F32)
    gate, up = projected[:, :FFE], projected[:, FFE:]
    hidden = (gate / (1.0 + jnp.exp(-gate)) * up).astype(BF16)
    out_ref[...] = jnp.dot(hidden, down_ref[0], preferred_element_type=F32).astype(BF16)


def expert(x, gate_up, down):
    rows, width = x.shape
    step = 256
    whole = lambda shape: pl.BlockSpec(
        shape, lambda i: (0,) * len(shape), pipeline_mode=pl.Buffered(1)
    )
    return pl.pallas_call(
        expert_kernel,
        grid=(rows // step,),
        in_specs=[
            pl.BlockSpec((step, width), lambda i: (i, 0)),
            whole(gate_up.shape),
            whole(down.shape),
        ],
        out_specs=pl.BlockSpec((step, width), lambda i: (i, 0)),
        out_shape=jax.ShapeDtypeStruct((rows, width), BF16),
        compiler_params=params(),
        name="expert",
    )(x, gate_up, down)


def combine_kernel(table_ref, rows_ref, *refs):
    before_ref, (out_ref, total_ref) = (refs[0] if len(refs) == 3 else None), refs[-2:]
    step = pl.program_id(0)
    tokens = out_ref.shape[0]
    part = lax.dot_general(table_ref[0], rows_ref[...], TN, preferred_element_type=F32)
    part = part[:tokens] + part[tokens:]

    @pl.when(step == 0)
    def _():
        total_ref[...] = part if before_ref is None else part + before_ref[...]

    @pl.when(step > 0)
    def _():
        total_ref[...] += part

    @pl.when(step == pl.num_programs(0) - 1)
    def _():
        out_ref[...] = total_ref[...].astype(out_ref.dtype)


def combine(table, rows, before, dtype, chunk):
    count, width = rows.shape
    tokens = table.shape[2] // 2
    step = 256
    whole = lambda shape: pl.BlockSpec(shape, lambda i: (0,) * len(shape))
    operands = (table, rows) + (() if before is None else (before,))
    return pl.pallas_call(
        combine_kernel,
        grid=(count // step,),
        in_specs=[
            pl.BlockSpec((1, step, 2 * tokens), lambda i: (chunk, i, 0)),
            pl.BlockSpec((step, width), lambda i: (i, 0)),
        ]
        + ([] if before is None else [whole(before.shape)]),
        out_specs=whole((tokens, width)),
        out_shape=jax.ShapeDtypeStruct((tokens, width), dtype),
        scratch_shapes=[pltpu.VMEM((tokens, width), F32)],
        compiler_params=params(),
        name="combine",
    )(*operands)


def fetch(packed, distance):
    shards = lax.axis_size("ctx")

    def back(by, block):
        return lax.ppermute(block, "ctx", [(i, i + by) for i in range(shards - by)])

    return lax.switch(
        distance - 1, [functools.partial(back, by) for by in range(1, shards)], packed
    )


def body(
    queries,
    keys,
    values,
    distances,
    out_weight,
    residual,
    norm_gain,
    expert_gate_up,
    expert_down,
    routes,
    route_weights,
):
    tokens, width = residual.shape
    devices = lax.axis_size(ALL)
    me, head = lax.axis_index("ctx"), lax.axis_index("head")
    place = jnp.stack([head, me])
    packed = jnp.stack([keys, values])
    far = [fetch(packed, distances[0, j]) for j in range(DIST)]
    send, table = tables(routes, route_weights, devices)
    own, one, two, three = attention(
        place, distances, queries, keys, values, far, out_weight
    )
    others = [
        lax.ppermute(a, "head", [(i, (i + r) % 4) for i in range(4)])
        for a, r in ((two, 2), (one, 1), (three, 3))
    ]
    attended, normed, first = norm_dispatch(own, others, residual, norm_gain, send)
    exchange = lambda a: lax.all_to_all(a, ALL, split_axis=0, concat_axis=0, tiled=True)
    arrived = [exchange(first)]
    for c in range(1, CHUNKS):
        arrived.append(exchange(dispatch(send, normed, c)))
    returned = [exchange(expert(a, expert_gate_up, expert_down)) for a in arrived]
    total = None
    for c in range(CHUNKS):
        total = combine(table, returned[c], total, BF16 if c == CHUNKS - 1 else F32, c)
    return (attended, total)


def solution(mesh):
    return jax.shard_map(
        body,
        mesh=mesh,
        in_specs=(
            P("ctx", "head"),
            P("ctx", "head"),
            P("ctx", "head"),
            P("head", None),
            P("head", None),
            P(ALL, None),
            P(),
            P(ALL, None, None),
            P(ALL, None, None),
            P(ALL, None),
            P(ALL, None),
        ),
        out_specs=(P(ALL, None), P(ALL, None)),
        check_vma=False,
    )
```

```python
import functools
import math

import jax
import jax.numpy as jnp
from jax import lax
from jax.experimental import pallas as pl
from jax.experimental.pallas import tpu as pltpu
from jax.sharding import PartitionSpec as P

HD = 128
FFE = 768
TOP = 8
BLK = 128
DIST = 3
CAP = 16
CHUNKS = 2
ALL = ("ctx", "head")
BF16 = jnp.bfloat16
F32 = jnp.float32
NT = (((1,), (1,)), ((), ()))
TN = (((0,), (0,)), ((), ()))
EXPONENT = math.log2(math.e) / math.sqrt(HD)
VMEM_LIMIT = 56 * 1024 * 1024


def params(steps=1):
    return pltpu.CompilerParams(
        dimension_semantics=("arbitrary",) * steps, vmem_limit_bytes=VMEM_LIMIT
    )


def attention_kernel(
    place, wanted, q_ref, k_ref, v_ref, far0_ref, far1_ref, far2_ref, weight_ref, *refs
):
    out_refs, (mixed_ref, w_ref, sem) = refs[:-3], refs[-3:]
    step = pl.program_id(0)
    steps = len(out_refs)
    blocks = k_ref.shape[0] // BLK
    heads = q_ref.shape[1] // HD
    block = place[1 + step]
    far_refs = (far0_ref, far1_ref, far2_ref)
    load = pltpu.make_async_copy(weight_ref, w_ref, sem)
    pl.when(step == 0)(load.start)

    def attend(at):
        near = at * BLK
        later = lax.broadcasted_iota(jnp.int32, (BLK, BLK), 0) > lax.broadcasted_iota(
            jnp.int32, (BLK, BLK), 1
        )
        bias = jnp.where(later, -jnp.inf, 0.0)
        bias = jnp.concatenate([bias] * heads, axis=1)
        reach = [jnp.where(place[0] >= wanted[0, j], 0.0, -jnp.inf) for j in range(DIST)]
        keys = jnp.concatenate([k_ref[: near + BLK]] + [r[0] for r in far_refs], axis=0)
        values = jnp.concatenate([v_ref[: near + BLK]] + [r[1] for r in far_refs], axis=0)
        query = jnp.concatenate([q_ref[:, n * HD : (n + 1) * HD] for n in range(heads)], axis=0)
        score = lax.dot_general(keys, query, NT, preferred_element_type=F32)
        parts = [score[:near]] if at else []
        parts.append(score[near : near + BLK] + bias)
        for j in range(DIST):
            start = near + (j + 1) * BLK
            parts.append(score[start : start + BLK] + reach[j])
        score = jnp.concatenate(parts, axis=0)
        highest = jnp.max(score, axis=0, keepdims=True)
        weight = jnp.exp2((score - highest) * EXPONENT)
        denominator = jnp.sum(weight, axis=0, keepdims=True)
        mixed = lax.dot_general(values, weight.astype(BF16), TN, preferred_element_type=F32)
        mixed = mixed / denominator
        for n in range(heads):
            mixed_ref[pl.ds(step * BLK, BLK), n * HD : (n + 1) * HD] = (
                mixed[:, n * BLK : (n + 1) * BLK].T.astype(BF16)
            )

    for at in range(blocks):
        pl.when(block == at)(functools.partial(attend, at))

    @pl.when(step == steps - 1)
    def _():
        load.wait()
        for i, out_ref in enumerate(out_refs):
            out_ref[...] = jnp.dot(
                mixed_ref[i * BLK : (i + 1) * BLK], w_ref[...], preferred_element_type=F32
            ).astype(BF16)


def attention(place, wanted, queries, keys, values, far, out_weight, steps):
    wide = queries.shape[1]
    width = out_weight.shape[1]
    at = lambda i, place: place[1 + i]
    whole = lambda shape: pl.BlockSpec(
        shape, lambda i, p, w: (0,) * len(shape), pipeline_mode=pl.Buffered(1)
    )
    return pl.pallas_call(
        attention_kernel,
        grid_spec=pltpu.PrefetchScalarGridSpec(
            num_scalar_prefetch=2,
            grid=(steps,),
            in_specs=[
                pl.BlockSpec((BLK, wide), lambda i, p, w: (at(i, p), 0)),
                whole(keys.shape),
                whole(values.shape),
            ]
            + [pl.BlockSpec((2, BLK, HD), lambda i, p, w: (0, at(i, p), 0))] * DIST
            + [pl.BlockSpec(memory_space=pl.ANY)],
            out_specs=(whole((BLK, width)),) * steps,
            scratch_shapes=[
                pltpu.VMEM((steps * BLK, wide), BF16),
                pltpu.VMEM(out_weight.shape, BF16),
                pltpu.SemaphoreType.DMA,
            ],
        ),
        out_shape=(jax.ShapeDtypeStruct((BLK, width), BF16),) * steps,
        compiler_params=params(),
        name="attention",
    )(place, wanted, queries, keys, values, *far, out_weight)


def tables_kernel(routes_ref, weights_ref, send_ref, table_ref, spread_ref):
    top, tokens = routes_ref.shape
    experts, slots = spread_ref.shape[:2]
    chunks = send_ref.shape[0]
    names = lax.broadcasted_iota(jnp.int32, (experts, tokens), 0)
    chosen = jnp.zeros((experts, tokens), F32)
    weight = jnp.zeros((experts, tokens), F32)
    for k in range(top):
        here = routes_ref[k : k + 1, :] == names
        chosen = jnp.where(here, 1.0, chosen)
        weight = jnp.where(here, weights_ref[k : k + 1, :], weight)
    before = (
        lax.broadcasted_iota(jnp.int32, (tokens, tokens), 0)
        < lax.broadcasted_iota(jnp.int32, (tokens, tokens), 1)
    ).astype(BF16)
    place = jnp.dot(chosen.astype(BF16), before, preferred_element_type=F32)
    place = jnp.where(chosen > 0.0, place, -1.0)
    high = weight.astype(BF16).astype(F32)
    low = weight - high

    def spread(c, value):
        for s in range(slots):
            spread_ref[:, s, :] = jnp.where(place == float(c * slots + s), value, 0.0)
        return spread_ref[...].reshape(experts * slots, tokens).astype(BF16)

    for c in range(chunks):
        send_ref[c] = spread(c, 1.0)
        table_ref[c, :, :tokens] = spread(c, high)
        table_ref[c, :, tokens:] = spread(c, low)


def tables(routes, route_weights, experts):
    tokens = routes.shape[0]
    slots = CAP // CHUNKS
    return pl.pallas_call(
        tables_kernel,
        out_shape=(
            jax.ShapeDtypeStruct((CHUNKS, experts * slots, tokens), BF16),
            jax.ShapeDtypeStruct((CHUNKS, experts * slots, 2 * tokens), BF16),
        ),
        scratch_shapes=[pltpu.VMEM((experts, slots, tokens), F32)],
        compiler_params=params(0),
        name="tables",
    )(routes.T, route_weights.T)


def norm_kernel(
    own_ref, r1_ref, r2_ref, r3_ref, residual_ref, gain_ref, send_ref, attended_ref, normed_ref, out_ref
):
    @pl.when(pl.program_id(0) == 0)
    def _():
        total = residual_ref[...].astype(F32) + own_ref[...].astype(F32)
        for part_ref in (r1_ref, r2_ref, r3_ref):
            total = total + part_ref[...].astype(F32)
        attended = total.astype(BF16)
        attended_ref[...] = attended
        wide = attended.astype(F32)
        inverse = lax.rsqrt(jnp.mean(wide * wide, axis=1, keepdims=True) + 1e-06)
        normed_ref[...] = (wide * inverse * gain_ref[...]).astype(BF16)

    out_ref[...] = jnp.dot(send_ref[0], normed_ref[...], preferred_element_type=F32).astype(BF16)


def norm_dispatch(own, others, residual, gain, send):
    tokens, width = residual.shape
    rows = send.shape[1]
    step = 512
    whole = lambda shape: pl.BlockSpec(shape, lambda i: (0,) * len(shape))
    return pl.pallas_call(
        norm_kernel,
        grid=(rows // step,),
        in_specs=[pl.BlockSpec(memory_space=pltpu.VMEM)] * 4
        + [whole((tokens, width)), whole((1, width)), pl.BlockSpec((1, step, tokens), lambda i: (0, i, 0))],
        out_specs=(
            whole((tokens, width)),
            whole((tokens, width)),
            pl.BlockSpec((step, width), lambda i: (i, 0)),
        ),
        out_shape=(
            jax.ShapeDtypeStruct((tokens, width), BF16),
            jax.ShapeDtypeStruct((tokens, width), BF16),
            jax.ShapeDtypeStruct((rows, width), BF16),
        ),
        compiler_params=params(),
        name="norm_dispatch",
    )(own, *others, residual, gain.reshape(1, width), send)


def dispatch_kernel(send_ref, normed_ref, out_ref):
    out_ref[...] = jnp.dot(send_ref[0], normed_ref[...], preferred_element_type=F32).astype(BF16)


def dispatch(send, normed, chunk):
    tokens, width = normed.shape
    rows = send.shape[1]
    step = 512
    return pl.pallas_call(
        dispatch_kernel,
        grid=(rows // step,),
        in_specs=[
            pl.BlockSpec((1, step, tokens), lambda i: (chunk, i, 0)),
            pl.BlockSpec((tokens, width), lambda i: (0, 0)),
        ],
        out_specs=pl.BlockSpec((step, width), lambda i: (i, 0)),
        out_shape=jax.ShapeDtypeStruct((rows, width), BF16),
        compiler_params=params(),
        name="dispatch",
    )(send, normed)


def expert_kernel(x_ref, gate_up_ref, down_ref, out_ref):
    projected = jnp.dot(x_ref[...], gate_up_ref[0], preferred_element_type=F32)
    gate, up = projected[:, :FFE], projected[:, FFE:]
    hidden = (gate / (1.0 + jnp.exp(-gate)) * up).astype(BF16)
    out_ref[...] = jnp.dot(hidden, down_ref[0], preferred_element_type=F32).astype(BF16)


def expert(x, gate_up, down):
    rows, width = x.shape
    step = 256
    whole = lambda shape: pl.BlockSpec(
        shape, lambda i: (0,) * len(shape), pipeline_mode=pl.Buffered(1)
    )
    return pl.pallas_call(
        expert_kernel,
        grid=(rows // step,),
        in_specs=[
            pl.BlockSpec((step, width), lambda i: (i, 0)),
            whole(gate_up.shape),
            whole(down.shape),
        ],
        out_specs=pl.BlockSpec((step, width), lambda i: (i, 0)),
        out_shape=jax.ShapeDtypeStruct((rows, width), BF16),
        compiler_params=params(),
        name="expert",
    )(x, gate_up, down)


def combine_kernel(table_ref, rows_ref, *refs):
    before_ref, (out_ref, total_ref) = (refs[0] if len(refs) == 3 else None), refs[-2:]
    step = pl.program_id(0)
    tokens = out_ref.shape[0]
    part = lax.dot_general(table_ref[0], rows_ref[...], TN, preferred_element_type=F32)
    part = part[:tokens] + part[tokens:]

    @pl.when(step == 0)
    def _():
        total_ref[...] = part if before_ref is None else part + before_ref[...]

    @pl.when(step > 0)
    def _():
        total_ref[...] += part

    @pl.when(step == pl.num_programs(0) - 1)
    def _():
        out_ref[...] = total_ref[...].astype(out_ref.dtype)


def combine(table, rows, before, dtype, chunk):
    count, width = rows.shape
    tokens = table.shape[2] // 2
    step = 512
    whole = lambda shape: pl.BlockSpec(shape, lambda i: (0,) * len(shape))
    operands = (table, rows) + (() if before is None else (before,))
    return pl.pallas_call(
        combine_kernel,
        grid=(count // step,),
        in_specs=[
            pl.BlockSpec((1, step, 2 * tokens), lambda i: (chunk, i, 0)),
            pl.BlockSpec((step, width), lambda i: (i, 0)),
        ]
        + ([] if before is None else [whole(before.shape)]),
        out_specs=whole((tokens, width)),
        out_shape=jax.ShapeDtypeStruct((tokens, width), dtype),
        scratch_shapes=[pltpu.VMEM((tokens, width), F32)],
        compiler_params=params(),
        name="combine",
    )(*operands)


def fetch(packed, distance):
    shards = lax.axis_size("ctx")

    def back(by, block):
        return lax.ppermute(block, "ctx", [(i, i + by) for i in range(shards - by)])

    return lax.switch(
        distance - 1, [functools.partial(back, by) for by in range(1, shards)], packed
    )


def body(
    queries,
    keys,
    values,
    distances,
    out_weight,
    residual,
    norm_gain,
    expert_gate_up,
    expert_down,
    routes,
    route_weights,
):
    tokens, width = residual.shape
    devices = lax.axis_size(ALL)
    me, head = lax.axis_index("ctx"), lax.axis_index("head")
    packed = jnp.stack([keys, values])
    far = [fetch(packed, distances[0, j]) for j in range(DIST)]
    send, table = tables(routes, route_weights, devices)
    group = lax.axis_size("head")

    def project(*relative):
        place = jnp.stack([me] + [lax.rem(head + r, group) for r in relative])
        return attention(
            place, distances, queries, keys, values, far, out_weight, len(relative)
        )

    def hand(block, by):
        return lax.ppermute(block, "head", [(i, (i + by) % group) for i in range(group)])

    (two,) = project(2)
    two = hand(two, 2)
    one, three, own = project(1, 3, 0)
    others = [two, hand(one, 1), hand(three, 3)]
    attended, normed, first = norm_dispatch(own, others, residual, norm_gain, send)
    exchange = lambda a: lax.all_to_all(a, ALL, split_axis=0, concat_axis=0, tiled=True)
    arrived = [exchange(first)]
    for c in range(1, CHUNKS):
        arrived.append(exchange(dispatch(send, normed, c)))
    returned = [exchange(expert(a, expert_gate_up, expert_down)) for a in arrived]
    total = None
    for c in range(CHUNKS):
        total = combine(table, returned[c], total, BF16 if c == CHUNKS - 1 else F32, c)
    return (attended, total)


def solution(mesh):
    return jax.shard_map(
        body,
        mesh=mesh,
        in_specs=(
            P("ctx", "head"),
            P("ctx", "head"),
            P("ctx", "head"),
            P("head", None),
            P("head", None),
            P(ALL, None),
            P(),
            P(ALL, None, None),
            P(ALL, None, None),
            P(ALL, None),
            P(ALL, None),
        ),
        out_specs=(P(ALL, None), P(ALL, None)),
        check_vma=False,
    )
```

```python
import functools
import math

import jax
import jax.numpy as jnp
from jax import lax
from jax.experimental import pallas as pl
from jax.experimental.pallas import tpu as pltpu
from jax.sharding import PartitionSpec as P

HD = 128
FFE = 768
TOP = 8
BLK = 128
DIST = 3
CAP = 16
CHUNKS = (8, 8)
ALL = ("ctx", "head")
BF16 = jnp.bfloat16
F32 = jnp.float32
NT = (((1,), (1,)), ((), ()))
TN = (((0,), (0,)), ((), ()))
EXPONENT = math.log2(math.e) / math.sqrt(HD)


def params(steps=1, limit=56):
    return pltpu.CompilerParams(
        dimension_semantics=("arbitrary",) * steps, vmem_limit_bytes=limit * 1024 * 1024
    )


def held(array):
    return pltpu.with_memory_space_constraint(array, pltpu.VMEM)


def attention_kernel(
    first, stride, place, wanted, q_ref, k_ref, v_ref, far0_ref, far1_ref, far2_ref, weight_ref, *refs
):
    out_refs, (mixed_ref, w_ref, sem) = refs[:-3], refs[-3:]
    step = pl.program_id(0)
    load = pltpu.make_async_copy(weight_ref, w_ref, sem)
    pl.when(step == 0)(load.start)
    steps = len(out_refs)
    blocks = k_ref.shape[0] // BLK
    heads = q_ref.shape[1] // HD
    block = lax.rem(place[1] + first + stride * step, blocks)
    far_refs = (far0_ref, far1_ref, far2_ref)

    def attend(at):
        near = at * BLK
        later = lax.broadcasted_iota(jnp.int32, (BLK, BLK), 0) > lax.broadcasted_iota(
            jnp.int32, (BLK, BLK), 1
        )
        bias = jnp.where(later, -jnp.inf, 0.0)
        bias = jnp.concatenate([bias] * heads, axis=1)
        reach = [jnp.where(place[0] >= wanted[0, j], 0.0, -jnp.inf) for j in range(DIST)]
        keys = jnp.concatenate([k_ref[: near + BLK]] + [r[0] for r in far_refs], axis=0)
        values = jnp.concatenate([v_ref[: near + BLK]] + [r[1] for r in far_refs], axis=0)
        query = jnp.concatenate([q_ref[:, n * HD : (n + 1) * HD] for n in range(heads)], axis=0)
        score = lax.dot_general(keys, query, NT, preferred_element_type=F32)
        parts = [score[:near]] if at else []
        parts.append(score[near : near + BLK] + bias)
        for j in range(DIST):
            start = near + (j + 1) * BLK
            parts.append(score[start : start + BLK] + reach[j])
        score = jnp.concatenate(parts, axis=0)
        highest = jnp.max(score, axis=0, keepdims=True)
        weight = jnp.exp2((score - highest) * EXPONENT)
        denominator = jnp.sum(weight, axis=0, keepdims=True)
        mixed = lax.dot_general(values, weight.astype(BF16), TN, preferred_element_type=F32)
        mixed = mixed / denominator
        for n in range(heads):
            mixed_ref[pl.ds(step * BLK, BLK), n * HD : (n + 1) * HD] = (
                mixed[:, n * BLK : (n + 1) * BLK].T.astype(BF16)
            )

    for at in range(blocks):
        pl.when(block == at)(functools.partial(attend, at))

    @pl.when(step == steps - 1)
    def _():
        load.wait()
        for i, out_ref in enumerate(out_refs):
            out_ref[...] = jnp.dot(
                mixed_ref[i * BLK : (i + 1) * BLK], w_ref[...], preferred_element_type=F32
            ).astype(BF16)


def attention(place, wanted, queries, keys, values, far, out_weight, first, stride, steps):
    length, wide = queries.shape
    width = out_weight.shape[1]
    at = lambda i, place: lax.rem(place[1] + first + stride * i, length // BLK)
    whole = lambda shape: pl.BlockSpec(
        shape, lambda i, p, w: (0,) * len(shape), pipeline_mode=pl.Buffered(1)
    )
    return pl.pallas_call(
        functools.partial(attention_kernel, first, stride),
        grid_spec=pltpu.PrefetchScalarGridSpec(
            num_scalar_prefetch=2,
            grid=(steps,),
            in_specs=[
                pl.BlockSpec((BLK, wide), lambda i, p, w: (at(i, p), 0)),
                whole(keys.shape),
                whole(values.shape),
            ]
            + [pl.BlockSpec((2, BLK, HD), lambda i, p, w: (0, at(i, p), 0))] * DIST
            + [pl.BlockSpec(memory_space=pl.ANY)],
            out_specs=(whole((BLK, width)),) * steps,
            scratch_shapes=[
                pltpu.VMEM((steps * BLK, wide), BF16),
                pltpu.VMEM(out_weight.shape, BF16),
                pltpu.SemaphoreType.DMA,
            ],
        ),
        out_shape=(jax.ShapeDtypeStruct((BLK, width), BF16),) * steps,
        compiler_params=params(),
        name="attention",
    )(place, wanted, queries, keys, values, *far, out_weight)


def tables_kernel(routes_ref, weights_ref, *refs):
    top, tokens = routes_ref.shape
    chunks = len(CHUNKS)
    send_refs, table_refs, spread_refs = refs[:chunks], refs[chunks : -chunks], refs[-chunks:]
    experts = spread_refs[0].shape[0]
    names = lax.broadcasted_iota(jnp.int32, (experts, tokens), 0)
    chosen = jnp.zeros((experts, tokens), F32)
    weight = jnp.zeros((experts, tokens), F32)
    for k in range(top):
        here = routes_ref[k : k + 1, :] == names
        chosen = jnp.where(here, 1.0, chosen)
        weight = jnp.where(here, weights_ref[k : k + 1, :], weight)
    before = (
        lax.broadcasted_iota(jnp.int32, (tokens, tokens), 0)
        < lax.broadcasted_iota(jnp.int32, (tokens, tokens), 1)
    ).astype(BF16)
    place = jnp.dot(chosen.astype(BF16), before, preferred_element_type=F32)
    place = jnp.where(chosen > 0.0, place, -1.0)
    high = weight.astype(BF16).astype(F32)
    low = weight - high

    first = 0
    for send_ref, table_ref, spread_ref, slots in zip(
        send_refs, table_refs, spread_refs, CHUNKS
    ):

        def spread(value):
            for s in range(slots):
                spread_ref[:, s, :] = jnp.where(place == float(first + s), value, 0.0)
            return spread_ref[...].reshape(experts * slots, tokens).astype(BF16)

        send_ref[...] = spread(1.0)
        table_ref[:, :tokens] = spread(high)
        table_ref[:, tokens:] = spread(low)
        first += slots


def tables(routes, route_weights, experts):
    tokens = routes.shape[0]
    shapes = lambda columns: tuple(
        jax.ShapeDtypeStruct((experts * slots, columns), BF16) for slots in CHUNKS
    )
    made = pl.pallas_call(
        tables_kernel,
        out_shape=shapes(tokens) + shapes(2 * tokens),
        scratch_shapes=[pltpu.VMEM((experts, slots, tokens), F32) for slots in CHUNKS],
        compiler_params=params(0),
        name="tables",
    )(routes.T, route_weights.T)
    return made[: len(CHUNKS)], made[len(CHUNKS) :]


def norm_kernel(
    own_ref, r1_ref, r2_ref, r3_ref, residual_ref, gain_ref, send_ref, attended_ref, normed_ref, out_ref
):
    @pl.when(pl.program_id(0) == 0)
    def _():
        total = residual_ref[...].astype(F32) + own_ref[...].astype(F32)
        for part_ref in (r1_ref, r2_ref, r3_ref):
            total = total + part_ref[...].astype(F32)
        attended = total.astype(BF16)
        attended_ref[...] = attended
        wide = attended.astype(F32)
        inverse = lax.rsqrt(jnp.mean(wide * wide, axis=1, keepdims=True) + 1e-06)
        normed_ref[...] = (wide * inverse * gain_ref[...]).astype(BF16)

    out_ref[...] = jnp.dot(send_ref[...], normed_ref[...], preferred_element_type=F32).astype(BF16)


def norm_dispatch(own, others, residual, gain, send):
    tokens, width = residual.shape
    rows = send.shape[0]
    step = 512
    whole = lambda shape: pl.BlockSpec(shape, lambda i: (0,) * len(shape))
    return pl.pallas_call(
        norm_kernel,
        grid=(rows // step,),
        in_specs=[whole((tokens, width))]
        + [pl.BlockSpec(memory_space=pltpu.VMEM)] * 3
        + [whole((tokens, width)), whole((1, width)), pl.BlockSpec((step, tokens), lambda i: (i, 0))],
        out_specs=(
            whole((tokens, width)),
            whole((tokens, width)),
            pl.BlockSpec((step, width), lambda i: (i, 0)),
        ),
        out_shape=(
            jax.ShapeDtypeStruct((tokens, width), BF16),
            jax.ShapeDtypeStruct((tokens, width), BF16),
            jax.ShapeDtypeStruct((rows, width), BF16),
        ),
        compiler_params=params(),
        name="norm_dispatch",
    )(own, *others, residual, gain.reshape(1, width), send)


def dispatch_kernel(send_ref, normed_ref, out_ref):
    out_ref[...] = jnp.dot(send_ref[...], normed_ref[...], preferred_element_type=F32).astype(BF16)


def dispatch(send, normed):
    tokens, width = normed.shape
    rows = send.shape[0]
    step = 512
    return pl.pallas_call(
        dispatch_kernel,
        grid=(rows // step,),
        in_specs=[
            pl.BlockSpec((step, tokens), lambda i: (i, 0)),
            pl.BlockSpec((tokens, width), lambda i: (0, 0)),
        ],
        out_specs=pl.BlockSpec((step, width), lambda i: (i, 0)),
        out_shape=jax.ShapeDtypeStruct((rows, width), BF16),
        compiler_params=params(),
        name="dispatch",
    )(send, normed)


def expert_kernel(x_ref, gate_up_ref, down_ref, out_ref):
    projected = jnp.dot(x_ref[...], gate_up_ref[0], preferred_element_type=F32)
    gate, up = projected[:, :FFE], projected[:, FFE:]
    hidden = (gate / (1.0 + jnp.exp(-gate)) * up).astype(BF16)
    out_ref[...] = jnp.dot(hidden, down_ref[0], preferred_element_type=F32).astype(BF16)


def expert(x, gate_up, down):
    rows, width = x.shape
    step = 256
    whole = lambda shape: pl.BlockSpec(
        shape, lambda i: (0,) * len(shape), pipeline_mode=pl.Buffered(1)
    )
    return pl.pallas_call(
        expert_kernel,
        grid=(rows // step,),
        in_specs=[
            pl.BlockSpec((step, width), lambda i: (i, 0)),
            whole(gate_up.shape),
            whole(down.shape),
        ],
        out_specs=pl.BlockSpec((step, width), lambda i: (i, 0)),
        out_shape=jax.ShapeDtypeStruct((rows, width), BF16),
        compiler_params=params(),
        name="expert",
    )(x, gate_up, down)


def combine_kernel(table_ref, rows_ref, *refs):
    before_ref, (out_ref, total_ref) = (refs[0] if len(refs) == 3 else None), refs[-2:]
    step = pl.program_id(0)
    tokens = out_ref.shape[0]
    part = lax.dot_general(table_ref[...], rows_ref[...], TN, preferred_element_type=F32)
    part = part[:tokens] + part[tokens:]

    @pl.when(step == 0)
    def _():
        total_ref[...] = part if before_ref is None else part + before_ref[...]

    @pl.when(step > 0)
    def _():
        total_ref[...] += part

    @pl.when(step == pl.num_programs(0) - 1)
    def _():
        out_ref[...] = total_ref[...].astype(out_ref.dtype)


def combine(table, rows, before, dtype):
    count, width = rows.shape
    tokens = table.shape[1] // 2
    step = 512
    whole = lambda shape: pl.BlockSpec(shape, lambda i: (0,) * len(shape))
    operands = (table, rows) + (() if before is None else (before,))
    return pl.pallas_call(
        combine_kernel,
        grid=(count // step,),
        in_specs=[
            pl.BlockSpec((step, 2 * tokens), lambda i: (i, 0)),
            pl.BlockSpec((step, width), lambda i: (i, 0)),
        ]
        + ([] if before is None else [whole(before.shape)]),
        out_specs=whole((tokens, width)),
        out_shape=jax.ShapeDtypeStruct((tokens, width), dtype),
        scratch_shapes=[pltpu.VMEM((tokens, width), F32)],
        compiler_params=params(),
        name="combine",
    )(*operands)


def fetch(packed, distance):
    shards = lax.axis_size("ctx")

    def back(by, block):
        return lax.ppermute(block, "ctx", [(i, i + by) for i in range(shards - by)])

    return lax.switch(
        distance - 1, [functools.partial(back, by) for by in range(1, shards)], packed
    )


def body(
    queries,
    keys,
    values,
    distances,
    out_weight,
    residual,
    norm_gain,
    expert_gate_up,
    expert_down,
    routes,
    route_weights,
):
    tokens, width = residual.shape
    devices = lax.axis_size(ALL)
    me, head = lax.axis_index("ctx"), lax.axis_index("head")
    packed = jnp.stack([keys, values])
    far = [fetch(packed, distances[0, j]) for j in range(DIST)]
    send, table = tables(routes, route_weights, devices)
    group = lax.axis_size("head")

    place = jnp.stack([me, head])

    def project(place, first, stride, steps):
        return attention(
            place, distances, queries, keys, values, far, out_weight, first, stride, steps
        )

    def hand(block, by):
        return lax.ppermute(block, "head", [(i, (i + by) % group) for i in range(group)])

    (two,) = project(place, 2, 1, 1)
    two, place = lax.optimization_barrier((two, place))
    two = hand(two, 2)
    one, three = project(place, 1, 2, 2)
    one, three, place = lax.optimization_barrier((one, three, place))
    others = [held(a) for a in (two, hand(one, 1), hand(three, 3))]
    (own,) = project(place, 0, 1, 1)
    attended, normed, first = norm_dispatch(own, others, residual, norm_gain, send[0])
    exchange = lambda a: lax.all_to_all(a, ALL, split_axis=0, concat_axis=0, tiled=True)
    arrived = [exchange(first)] + [exchange(dispatch(s, normed)) for s in send[1:]]
    returned = [exchange(expert(a, expert_gate_up, expert_down)) for a in arrived]
    total = None
    for c, (t, r) in enumerate(zip(table, returned)):
        total = combine(t, r, total, BF16 if c == len(CHUNKS) - 1 else F32)
    return (attended, total)


def solution(mesh):
    return jax.shard_map(
        body,
        mesh=mesh,
        in_specs=(
            P("ctx", "head"),
            P("ctx", "head"),
            P("ctx", "head"),
            P("head", None),
            P("head", None),
            P(ALL, None),
            P(),
            P(ALL, None, None),
            P(ALL, None, None),
            P(ALL, None),
            P(ALL, None),
        ),
        out_specs=(P(ALL, None), P(ALL, None)),
        check_vma=False,
    )
```

```python
import functools
import math

import jax
import jax.numpy as jnp
from jax import lax
from jax.experimental import pallas as pl
from jax.experimental.pallas import tpu as pltpu
from jax.sharding import PartitionSpec as P

HD = 128
FFE = 768
TOP = 8
BLK = 128
DIST = 3
CAP = 16
CHUNKS = (8, 8)
ALL = ("ctx", "head")
BF16 = jnp.bfloat16
F32 = jnp.float32
NT = (((1,), (1,)), ((), ()))
TN = (((0,), (0,)), ((), ()))
EXPONENT = math.log2(math.e) / math.sqrt(HD)


def params(steps=1, limit=56):
    return pltpu.CompilerParams(
        dimension_semantics=("arbitrary",) * steps, vmem_limit_bytes=limit * 1024 * 1024
    )


def held(array):
    return pltpu.with_memory_space_constraint(array, pltpu.VMEM)


def attention_kernel(
    first, stride, place, wanted, q_ref, k_ref, v_ref, far_ref, weight_ref, *refs
):
    out_refs, (mixed_ref, w_ref, sem) = refs[:-3], refs[-3:]
    step = pl.program_id(0)
    load = pltpu.make_async_copy(weight_ref, w_ref, sem)
    pl.when(step == 0)(load.start)
    steps = len(out_refs)
    blocks = k_ref.shape[0] // BLK
    heads = q_ref.shape[1] // HD
    block = lax.rem(place[1] + first + stride * step, blocks)

    def attend(at):
        near = at * BLK
        later = lax.broadcasted_iota(jnp.int32, (BLK, BLK), 0) > lax.broadcasted_iota(
            jnp.int32, (BLK, BLK), 1
        )
        bias = jnp.where(later, -jnp.inf, 0.0)
        bias = jnp.concatenate([bias] * heads, axis=1)
        reach = [jnp.where(place[0] >= wanted[0, j], 0.0, -jnp.inf) for j in range(DIST)]
        keys = jnp.concatenate([k_ref[: near + BLK]] + [far_ref[j, 0] for j in range(DIST)], axis=0)
        values = jnp.concatenate([v_ref[: near + BLK]] + [far_ref[j, 1] for j in range(DIST)], axis=0)
        query = jnp.concatenate([q_ref[:, n * HD : (n + 1) * HD] for n in range(heads)], axis=0)
        score = lax.dot_general(keys, query, NT, preferred_element_type=F32)
        parts = [score[:near]] if at else []
        parts.append(score[near : near + BLK] + bias)
        for j in range(DIST):
            start = near + (j + 1) * BLK
            parts.append(score[start : start + BLK] + reach[j])
        score = jnp.concatenate(parts, axis=0)
        highest = jnp.max(score, axis=0, keepdims=True)
        weight = jnp.exp2((score - highest) * EXPONENT)
        denominator = jnp.sum(weight, axis=0, keepdims=True)
        mixed = lax.dot_general(values, weight.astype(BF16), TN, preferred_element_type=F32)
        mixed = mixed / denominator
        for n in range(heads):
            mixed_ref[pl.ds(step * BLK, BLK), n * HD : (n + 1) * HD] = (
                mixed[:, n * BLK : (n + 1) * BLK].T.astype(BF16)
            )

    for at in range(blocks):
        pl.when(block == at)(functools.partial(attend, at))

    @pl.when(step == steps - 1)
    def _():
        load.wait()
        for i, out_ref in enumerate(out_refs):
            out_ref[...] = jnp.dot(
                mixed_ref[i * BLK : (i + 1) * BLK], w_ref[...], preferred_element_type=F32
            ).astype(BF16)


def attention(place, wanted, queries, keys, values, far, out_weight, first, stride, steps):
    length, wide = queries.shape
    width = out_weight.shape[1]
    at = lambda i, place: lax.rem(place[1] + first + stride * i, length // BLK)
    whole = lambda shape: pl.BlockSpec(
        shape, lambda i, p, w: (0,) * len(shape), pipeline_mode=pl.Buffered(1)
    )
    return pl.pallas_call(
        functools.partial(attention_kernel, first, stride),
        grid_spec=pltpu.PrefetchScalarGridSpec(
            num_scalar_prefetch=2,
            grid=(steps,),
            in_specs=[
                pl.BlockSpec((BLK, wide), lambda i, p, w: (at(i, p), 0)),
                whole(keys.shape),
                whole(values.shape),
            ]
            + [pl.BlockSpec((DIST, 2, BLK, HD), lambda i, p, w: (0, 0, at(i, p), 0))]
            + [pl.BlockSpec(memory_space=pl.ANY)],
            out_specs=(whole((BLK, width)),) * steps,
            scratch_shapes=[
                pltpu.VMEM((steps * BLK, wide), BF16),
                pltpu.VMEM(out_weight.shape, BF16),
                pltpu.SemaphoreType.DMA,
            ],
        ),
        out_shape=(jax.ShapeDtypeStruct((BLK, width), BF16),) * steps,
        compiler_params=params(),
        name="attention",
    )(place, wanted, queries, keys, values, far, out_weight)


def tables_kernel(routes_ref, weights_ref, *refs):
    top, tokens = routes_ref.shape
    chunks = len(CHUNKS)
    send_refs, table_refs, spread_refs = refs[:chunks], refs[chunks : -chunks], refs[-chunks:]
    experts = spread_refs[0].shape[0]
    names = lax.broadcasted_iota(jnp.int32, (experts, tokens), 0)
    chosen = jnp.zeros((experts, tokens), F32)
    weight = jnp.zeros((experts, tokens), F32)
    for k in range(top):
        here = routes_ref[k : k + 1, :] == names
        chosen = jnp.where(here, 1.0, chosen)
        weight = jnp.where(here, weights_ref[k : k + 1, :], weight)
    before = (
        lax.broadcasted_iota(jnp.int32, (tokens, tokens), 0)
        < lax.broadcasted_iota(jnp.int32, (tokens, tokens), 1)
    ).astype(BF16)
    place = jnp.dot(chosen.astype(BF16), before, preferred_element_type=F32)
    place = jnp.where(chosen > 0.0, place, -1.0)
    high = weight.astype(BF16).astype(F32)
    low = weight - high

    first = 0
    for send_ref, table_ref, spread_ref, slots in zip(
        send_refs, table_refs, spread_refs, CHUNKS
    ):

        def spread(value):
            for s in range(slots):
                spread_ref[:, s, :] = jnp.where(place == float(first + s), value, 0.0)
            return spread_ref[...].reshape(experts * slots, tokens).astype(BF16)

        send_ref[...] = spread(1.0)
        table_ref[:, :tokens] = spread(high)
        table_ref[:, tokens:] = spread(low)
        first += slots


def tables(routes, route_weights, experts):
    tokens = routes.shape[0]
    shapes = lambda columns: tuple(
        jax.ShapeDtypeStruct((experts * slots, columns), BF16) for slots in CHUNKS
    )
    made = pl.pallas_call(
        tables_kernel,
        out_shape=shapes(tokens) + shapes(2 * tokens),
        scratch_shapes=[pltpu.VMEM((experts, slots, tokens), F32) for slots in CHUNKS],
        compiler_params=params(0),
        name="tables",
    )(routes.T, route_weights.T)
    return made[: len(CHUNKS)], made[len(CHUNKS) :]


def norm_kernel(
    own_ref, r1_ref, r2_ref, r3_ref, residual_ref, gain_ref, send_ref, attended_ref, normed_ref, out_ref
):
    @pl.when(pl.program_id(0) == 0)
    def _():
        total = residual_ref[...].astype(F32) + own_ref[...].astype(F32)
        for part_ref in (r1_ref, r2_ref, r3_ref):
            total = total + part_ref[...].astype(F32)
        attended = total.astype(BF16)
        attended_ref[...] = attended
        wide = attended.astype(F32)
        inverse = lax.rsqrt(jnp.mean(wide * wide, axis=1, keepdims=True) + 1e-06)
        normed_ref[...] = (wide * inverse * gain_ref[...]).astype(BF16)

    out_ref[...] = jnp.dot(send_ref[...], normed_ref[...], preferred_element_type=F32).astype(BF16)


def norm_dispatch(own, others, residual, gain, send):
    tokens, width = residual.shape
    rows = send.shape[0]
    step = 512
    whole = lambda shape: pl.BlockSpec(shape, lambda i: (0,) * len(shape))
    return pl.pallas_call(
        norm_kernel,
        grid=(rows // step,),
        in_specs=[whole((tokens, width))]
        + [pl.BlockSpec(memory_space=pltpu.VMEM)] * 3
        + [whole((tokens, width)), whole((1, width)), pl.BlockSpec((step, tokens), lambda i: (i, 0))],
        out_specs=(
            whole((tokens, width)),
            whole((tokens, width)),
            pl.BlockSpec((step, width), lambda i: (i, 0)),
        ),
        out_shape=(
            jax.ShapeDtypeStruct((tokens, width), BF16),
            jax.ShapeDtypeStruct((tokens, width), BF16),
            jax.ShapeDtypeStruct((rows, width), BF16),
        ),
        compiler_params=params(),
        name="norm_dispatch",
    )(own, *others, residual, gain.reshape(1, width), send)


def dispatch_kernel(send_ref, normed_ref, out_ref):
    out_ref[...] = jnp.dot(send_ref[...], normed_ref[...], preferred_element_type=F32).astype(BF16)


def dispatch(send, normed):
    tokens, width = normed.shape
    rows = send.shape[0]
    step = 512
    return pl.pallas_call(
        dispatch_kernel,
        grid=(rows // step,),
        in_specs=[
            pl.BlockSpec((step, tokens), lambda i: (i, 0)),
            pl.BlockSpec((tokens, width), lambda i: (0, 0)),
        ],
        out_specs=pl.BlockSpec((step, width), lambda i: (i, 0)),
        out_shape=jax.ShapeDtypeStruct((rows, width), BF16),
        compiler_params=params(),
        name="dispatch",
    )(send, normed)


def expert_kernel(x_ref, gate_up_ref, down_ref, out_ref):
    projected = jnp.dot(x_ref[...], gate_up_ref[0], preferred_element_type=F32)
    gate, up = projected[:, :FFE], projected[:, FFE:]
    hidden = (gate / (1.0 + jnp.exp(-gate)) * up).astype(BF16)
    out_ref[...] = jnp.dot(hidden, down_ref[0], preferred_element_type=F32).astype(BF16)


def expert(x, gate_up, down):
    rows, width = x.shape
    step = 256
    whole = lambda shape: pl.BlockSpec(
        shape, lambda i: (0,) * len(shape), pipeline_mode=pl.Buffered(1)
    )
    return pl.pallas_call(
        expert_kernel,
        grid=(rows // step,),
        in_specs=[
            pl.BlockSpec((step, width), lambda i: (i, 0)),
            whole(gate_up.shape),
            whole(down.shape),
        ],
        out_specs=pl.BlockSpec((step, width), lambda i: (i, 0)),
        out_shape=jax.ShapeDtypeStruct((rows, width), BF16),
        compiler_params=params(),
        name="expert",
    )(x, gate_up, down)


def combine_kernel(table_ref, rows_ref, *refs):
    before_ref, (out_ref, total_ref) = (refs[0] if len(refs) == 3 else None), refs[-2:]
    step = pl.program_id(0)
    tokens = out_ref.shape[0]
    part = lax.dot_general(table_ref[...], rows_ref[...], TN, preferred_element_type=F32)
    part = part[:tokens] + part[tokens:]

    @pl.when(step == 0)
    def _():
        total_ref[...] = part if before_ref is None else part + before_ref[...]

    @pl.when(step > 0)
    def _():
        total_ref[...] += part

    @pl.when(step == pl.num_programs(0) - 1)
    def _():
        out_ref[...] = total_ref[...].astype(out_ref.dtype)


def combine(table, rows, before, dtype):
    count, width = rows.shape
    tokens = table.shape[1] // 2
    step = 512
    whole = lambda shape: pl.BlockSpec(shape, lambda i: (0,) * len(shape))
    operands = (table, rows) + (() if before is None else (before,))
    return pl.pallas_call(
        combine_kernel,
        grid=(count // step,),
        in_specs=[
            pl.BlockSpec((step, 2 * tokens), lambda i: (i, 0)),
            pl.BlockSpec((step, width), lambda i: (i, 0)),
        ]
        + ([] if before is None else [whole(before.shape)]),
        out_specs=whole((tokens, width)),
        out_shape=jax.ShapeDtypeStruct((tokens, width), dtype),
        scratch_shapes=[pltpu.VMEM((tokens, width), F32)],
        compiler_params=params(),
        name="combine",
    )(*operands)


def fetch(packed, distance):
    shards = lax.axis_size("ctx")

    def back(by, block):
        return lax.ppermute(block, "ctx", [(i, i + by) for i in range(shards - by)])

    return lax.switch(
        distance - 1, [functools.partial(back, by) for by in range(1, shards)], packed
    )


def body(
    queries,
    keys,
    values,
    distances,
    out_weight,
    residual,
    norm_gain,
    expert_gate_up,
    expert_down,
    routes,
    route_weights,
):
    tokens, width = residual.shape
    devices = lax.axis_size(ALL)
    me, head = lax.axis_index("ctx"), lax.axis_index("head")
    packed = jnp.stack([keys, values])
    far = lax.fori_loop(
        0,
        DIST,
        lambda j, kept: lax.dynamic_update_index_in_dim(
            kept, fetch(packed, lax.dynamic_index_in_dim(distances[0], j, 0, False)), j, 0
        ),
        jnp.zeros((DIST,) + packed.shape, BF16),
    )
    send, table = tables(routes, route_weights, devices)
    group = lax.axis_size("head")

    place = jnp.stack([me, head])

    def project(place, first, stride, steps):
        return attention(
            place, distances, queries, keys, values, far, out_weight, first, stride, steps
        )

    def hand(block, by):
        return lax.ppermute(block, "head", [(i, (i + by) % group) for i in range(group)])

    (two,) = project(place, 2, 1, 1)
    two, place = lax.optimization_barrier((two, place))
    two = hand(two, 2)
    one, three = project(place, 1, 2, 2)
    one, three, place = lax.optimization_barrier((one, three, place))
    others = [held(a) for a in (two, hand(one, 1), hand(three, 3))]
    (own,) = project(place, 0, 1, 1)
    attended, normed, first = norm_dispatch(own, others, residual, norm_gain, send[0])
    exchange = lambda a: lax.all_to_all(a, ALL, split_axis=0, concat_axis=0, tiled=True)
    arrived = [exchange(first)] + [exchange(dispatch(s, normed)) for s in send[1:]]
    returned = [exchange(expert(a, expert_gate_up, expert_down)) for a in arrived]
    total = None
    for c, (t, r) in enumerate(zip(table, returned)):
        total = combine(t, r, total, BF16 if c == len(CHUNKS) - 1 else F32)
    return (attended, total)


def solution(mesh):
    return jax.shard_map(
        body,
        mesh=mesh,
        in_specs=(
            P("ctx", "head"),
            P("ctx", "head"),
            P("ctx", "head"),
            P("head", None),
            P("head", None),
            P(ALL, None),
            P(),
            P(ALL, None, None),
            P(ALL, None, None),
            P(ALL, None),
            P(ALL, None),
        ),
        out_specs=(P(ALL, None), P(ALL, None)),
        check_vma=False,
    )
```

```python
import functools
import math

import jax
import jax.numpy as jnp
from jax import lax
from jax.experimental import pallas as pl
from jax.experimental.pallas import tpu as pltpu
from jax.sharding import PartitionSpec as P

HD = 128
FFE = 768
TOP = 8
BLK = 128
DIST = 3
CAP = 16
CHUNKS = (8, 8)
ALL = ("ctx", "head")
BF16 = jnp.bfloat16
F32 = jnp.float32
NT = (((1,), (1,)), ((), ()))
TN = (((0,), (0,)), ((), ()))
EXPONENT = math.log2(math.e) / math.sqrt(HD)


def params(steps=1, limit=56):
    return pltpu.CompilerParams(
        dimension_semantics=("arbitrary",) * steps, vmem_limit_bytes=limit * 1024 * 1024
    )


def held(array):
    return pltpu.with_memory_space_constraint(array, pltpu.VMEM)


def attention_kernel(
    first, stride, place, wanted, q_ref, k_ref, v_ref, far0_ref, far1_ref, far2_ref, weight_ref, *refs
):
    out_refs, (mixed_ref, w_ref, sem) = refs[:-3], refs[-3:]
    step = pl.program_id(0)
    load = pltpu.make_async_copy(weight_ref, w_ref, sem)
    pl.when(step == 0)(load.start)
    steps = len(out_refs)
    blocks = k_ref.shape[0] // BLK
    heads = q_ref.shape[1] // HD
    block = lax.rem(place[1] + first + stride * step, blocks)
    far_refs = (far0_ref, far1_ref, far2_ref)

    def attend(wide):
        rows = lax.broadcasted_iota(jnp.int32, (2 * BLK, BLK), 0)
        columns = lax.broadcasted_iota(jnp.int32, (2 * BLK, BLK), 1)
        bias = jnp.where(rows > columns + lax.rem(block, 2) * BLK, -jnp.inf, 0.0)
        bias = jnp.concatenate([bias] * heads, axis=1)
        reach = [jnp.where(place[0] >= wanted[0, j], 0.0, -jnp.inf) for j in range(DIST)]
        keys = jnp.concatenate([k_ref[:wide]] + [r[0] for r in far_refs], axis=0)
        values = jnp.concatenate([v_ref[:wide]] + [r[1] for r in far_refs], axis=0)
        query = jnp.concatenate([q_ref[:, n * HD : (n + 1) * HD] for n in range(heads)], axis=0)
        score = lax.dot_general(keys, query, NT, preferred_element_type=F32)
        early = wide - 2 * BLK
        parts = [score[:early]] if early else []
        parts.append(score[early:wide] + bias)
        for j in range(DIST):
            parts.append(score[wide + j * BLK : wide + (j + 1) * BLK] + reach[j])
        score = jnp.concatenate(parts, axis=0)
        highest = jnp.max(score, axis=0, keepdims=True)
        weight = jnp.exp2((score - highest) * EXPONENT)
        denominator = jnp.sum(weight, axis=0, keepdims=True)
        mixed = lax.dot_general(values, weight.astype(BF16), TN, preferred_element_type=F32)
        mixed = mixed / denominator
        for n in range(heads):
            mixed_ref[pl.ds(step * BLK, BLK), n * HD : (n + 1) * HD] = (
                mixed[:, n * BLK : (n + 1) * BLK].T.astype(BF16)
            )

    for pair in range(blocks // 2):
        pl.when(block // 2 == pair)(functools.partial(attend, 2 * BLK * (pair + 1)))

    @pl.when(step == steps - 1)
    def _():
        load.wait()
        for i, out_ref in enumerate(out_refs):
            out_ref[...] = jnp.dot(
                mixed_ref[i * BLK : (i + 1) * BLK], w_ref[...], preferred_element_type=F32
            ).astype(BF16)


def attention(place, wanted, queries, keys, values, far, out_weight, first, stride, steps):
    length, wide = queries.shape
    width = out_weight.shape[1]
    at = lambda i, place: lax.rem(place[1] + first + stride * i, length // BLK)
    whole = lambda shape: pl.BlockSpec(
        shape, lambda i, p, w: (0,) * len(shape), pipeline_mode=pl.Buffered(1)
    )
    return pl.pallas_call(
        functools.partial(attention_kernel, first, stride),
        grid_spec=pltpu.PrefetchScalarGridSpec(
            num_scalar_prefetch=2,
            grid=(steps,),
            in_specs=[
                pl.BlockSpec((BLK, wide), lambda i, p, w: (at(i, p), 0)),
                whole(keys.shape),
                whole(values.shape),
            ]
            + [pl.BlockSpec((2, BLK, HD), lambda i, p, w: (0, at(i, p), 0))] * DIST
            + [pl.BlockSpec(memory_space=pl.ANY)],
            out_specs=(whole((BLK, width)),) * steps,
            scratch_shapes=[
                pltpu.VMEM((steps * BLK, wide), BF16),
                pltpu.VMEM(out_weight.shape, BF16),
                pltpu.SemaphoreType.DMA,
            ],
        ),
        out_shape=(jax.ShapeDtypeStruct((BLK, width), BF16),) * steps,
        compiler_params=params(),
        name="attention",
    )(place, wanted, queries, keys, values, *far, out_weight)


def tables_kernel(routes_ref, weights_ref, *refs):
    top, tokens = routes_ref.shape
    chunks = len(CHUNKS)
    send_refs, table_refs, spread_refs = refs[:chunks], refs[chunks : -chunks], refs[-chunks:]
    experts = spread_refs[0].shape[0]
    names = lax.broadcasted_iota(jnp.int32, (experts, tokens), 0)
    chosen = jnp.zeros((experts, tokens), F32)
    weight = jnp.zeros((experts, tokens), F32)
    for k in range(top):
        here = routes_ref[k : k + 1, :] == names
        chosen = jnp.where(here, 1.0, chosen)
        weight = jnp.where(here, weights_ref[k : k + 1, :], weight)
    before = (
        lax.broadcasted_iota(jnp.int32, (tokens, tokens), 0)
        < lax.broadcasted_iota(jnp.int32, (tokens, tokens), 1)
    ).astype(BF16)
    place = jnp.dot(chosen.astype(BF16), before, preferred_element_type=F32)
    place = jnp.where(chosen > 0.0, place, -1.0)
    high = weight.astype(BF16).astype(F32)
    low = weight - high

    first = 0
    for send_ref, table_ref, spread_ref, slots in zip(
        send_refs, table_refs, spread_refs, CHUNKS
    ):

        def spread(value):
            for s in range(slots):
                spread_ref[:, s, :] = jnp.where(place == float(first + s), value, 0.0)
            return spread_ref[...].reshape(experts * slots, tokens).astype(BF16)

        send_ref[...] = spread(1.0)
        table_ref[:, :tokens] = spread(high)
        table_ref[:, tokens:] = spread(low)
        first += slots


def tables(routes, route_weights, experts):
    tokens = routes.shape[0]
    shapes = lambda columns: tuple(
        jax.ShapeDtypeStruct((experts * slots, columns), BF16) for slots in CHUNKS
    )
    made = pl.pallas_call(
        tables_kernel,
        out_shape=shapes(tokens) + shapes(2 * tokens),
        scratch_shapes=[pltpu.VMEM((experts, slots, tokens), F32) for slots in CHUNKS],
        compiler_params=params(0),
        name="tables",
    )(routes.T, route_weights.T)
    return made[: len(CHUNKS)], made[len(CHUNKS) :]


def norm_kernel(
    own_ref, r1_ref, r2_ref, r3_ref, residual_ref, gain_ref, send_ref, attended_ref, normed_ref, out_ref
):
    @pl.when(pl.program_id(0) == 0)
    def _():
        total = residual_ref[...].astype(F32) + own_ref[...].astype(F32)
        for part_ref in (r1_ref, r2_ref, r3_ref):
            total = total + part_ref[...].astype(F32)
        attended = total.astype(BF16)
        attended_ref[...] = attended
        wide = attended.astype(F32)
        inverse = lax.rsqrt(jnp.mean(wide * wide, axis=1, keepdims=True) + 1e-06)
        normed_ref[...] = (wide * inverse * gain_ref[...]).astype(BF16)

    out_ref[...] = jnp.dot(send_ref[...], normed_ref[...], preferred_element_type=F32).astype(BF16)


def norm_dispatch(own, others, residual, gain, send):
    tokens, width = residual.shape
    rows = send.shape[0]
    step = 512
    whole = lambda shape: pl.BlockSpec(shape, lambda i: (0,) * len(shape))
    return pl.pallas_call(
        norm_kernel,
        grid=(rows // step,),
        in_specs=[whole((tokens, width))]
        + [pl.BlockSpec(memory_space=pltpu.VMEM)] * 3
        + [whole((tokens, width)), whole((1, width)), pl.BlockSpec((step, tokens), lambda i: (i, 0))],
        out_specs=(
            whole((tokens, width)),
            whole((tokens, width)),
            pl.BlockSpec((step, width), lambda i: (i, 0)),
        ),
        out_shape=(
            jax.ShapeDtypeStruct((tokens, width), BF16),
            jax.ShapeDtypeStruct((tokens, width), BF16),
            jax.ShapeDtypeStruct((rows, width), BF16),
        ),
        compiler_params=params(),
        name="norm_dispatch",
    )(own, *others, residual, gain.reshape(1, width), send)


def dispatch_kernel(send_ref, normed_ref, out_ref):
    out_ref[...] = jnp.dot(send_ref[...], normed_ref[...], preferred_element_type=F32).astype(BF16)


def dispatch(send, normed):
    tokens, width = normed.shape
    rows = send.shape[0]
    step = 512
    return pl.pallas_call(
        dispatch_kernel,
        grid=(rows // step,),
        in_specs=[
            pl.BlockSpec((step, tokens), lambda i: (i, 0)),
            pl.BlockSpec((tokens, width), lambda i: (0, 0)),
        ],
        out_specs=pl.BlockSpec((step, width), lambda i: (i, 0)),
        out_shape=jax.ShapeDtypeStruct((rows, width), BF16),
        compiler_params=params(),
        name="dispatch",
    )(send, normed)


def expert_kernel(x_ref, gate_up_ref, down_ref, out_ref):
    projected = jnp.dot(x_ref[...], gate_up_ref[0], preferred_element_type=F32)
    gate, up = projected[:, :FFE], projected[:, FFE:]
    hidden = (gate / (1.0 + jnp.exp(-gate)) * up).astype(BF16)
    out_ref[...] = jnp.dot(hidden, down_ref[0], preferred_element_type=F32).astype(BF16)


def expert(x, gate_up, down):
    rows, width = x.shape
    step = 256
    whole = lambda shape: pl.BlockSpec(
        shape, lambda i: (0,) * len(shape), pipeline_mode=pl.Buffered(1)
    )
    return pl.pallas_call(
        expert_kernel,
        grid=(rows // step,),
        in_specs=[
            pl.BlockSpec((step, width), lambda i: (i, 0)),
            whole(gate_up.shape),
            whole(down.shape),
        ],
        out_specs=pl.BlockSpec((step, width), lambda i: (i, 0)),
        out_shape=jax.ShapeDtypeStruct((rows, width), BF16),
        compiler_params=params(),
        name="expert",
    )(x, gate_up, down)


def combine_kernel(table_ref, rows_ref, *refs):
    before_ref, (out_ref, total_ref) = (refs[0] if len(refs) == 3 else None), refs[-2:]
    step = pl.program_id(0)
    tokens = out_ref.shape[0]
    part = lax.dot_general(table_ref[...], rows_ref[...], TN, preferred_element_type=F32)
    part = part[:tokens] + part[tokens:]

    @pl.when(step == 0)
    def _():
        total_ref[...] = part if before_ref is None else part + before_ref[...]

    @pl.when(step > 0)
    def _():
        total_ref[...] += part

    @pl.when(step == pl.num_programs(0) - 1)
    def _():
        out_ref[...] = total_ref[...].astype(out_ref.dtype)


def combine(table, rows, before, dtype):
    count, width = rows.shape
    tokens = table.shape[1] // 2
    step = 512
    whole = lambda shape: pl.BlockSpec(shape, lambda i: (0,) * len(shape))
    operands = (table, rows) + (() if before is None else (before,))
    return pl.pallas_call(
        combine_kernel,
        grid=(count // step,),
        in_specs=[
            pl.BlockSpec((step, 2 * tokens), lambda i: (i, 0)),
            pl.BlockSpec((step, width), lambda i: (i, 0)),
        ]
        + ([] if before is None else [whole(before.shape)]),
        out_specs=whole((tokens, width)),
        out_shape=jax.ShapeDtypeStruct((tokens, width), dtype),
        scratch_shapes=[pltpu.VMEM((tokens, width), F32)],
        compiler_params=params(),
        name="combine",
    )(*operands)


def fetch(packed, distance):
    shards = lax.axis_size("ctx")

    def back(by, block):
        return lax.ppermute(block, "ctx", [(i, i + by) for i in range(shards - by)])

    return lax.switch(
        distance,
        [lambda block: block] + [functools.partial(back, by) for by in range(1, shards)],
        packed,
    )


def body(
    queries,
    keys,
    values,
    distances,
    out_weight,
    residual,
    norm_gain,
    expert_gate_up,
    expert_down,
    routes,
    route_weights,
):
    tokens, width = residual.shape
    devices = lax.axis_size(ALL)
    me, head = lax.axis_index("ctx"), lax.axis_index("head")
    packed = jnp.stack([keys, values])
    far = [fetch(packed, distances[0, j]) for j in range(DIST)]
    send, table = tables(routes, route_weights, devices)
    group = lax.axis_size("head")

    place = jnp.stack([me, head])

    def project(place, first, stride, steps):
        return attention(
            place, distances, queries, keys, values, far, out_weight, first, stride, steps
        )

    def hand(block, by):
        return lax.ppermute(block, "head", [(i, (i + by) % group) for i in range(group)])

    (two,) = project(place, 2, 1, 1)
    two, place = lax.optimization_barrier((two, place))
    two = hand(two, 2)
    one, three = project(place, 1, 2, 2)
    one, three, place = lax.optimization_barrier((one, three, place))
    others = [held(a) for a in (two, hand(one, 1), hand(three, 3))]
    (own,) = project(place, 0, 1, 1)
    attended, normed, first = norm_dispatch(own, others, residual, norm_gain, send[0])
    exchange = lambda a: lax.all_to_all(a, ALL, split_axis=0, concat_axis=0, tiled=True)
    arrived = [exchange(first)] + [exchange(dispatch(s, normed)) for s in send[1:]]
    returned = [exchange(expert(a, expert_gate_up, expert_down)) for a in arrived]
    total = None
    for c, (t, r) in enumerate(zip(table, returned)):
        total = combine(t, r, total, BF16 if c == len(CHUNKS) - 1 else F32)
    return (attended, total)


def solution(mesh):
    return jax.shard_map(
        body,
        mesh=mesh,
        in_specs=(
            P("ctx", "head"),
            P("ctx", "head"),
            P("ctx", "head"),
            P("head", None),
            P("head", None),
            P(ALL, None),
            P(),
            P(ALL, None, None),
            P(ALL, None, None),
            P(ALL, None),
            P(ALL, None),
        ),
        out_specs=(P(ALL, None), P(ALL, None)),
        check_vma=False,
    )
```

```python
import functools
import math

import jax
import jax.numpy as jnp
from jax import lax
from jax.experimental import pallas as pl
from jax.experimental.pallas import tpu as pltpu
from jax.sharding import PartitionSpec as P

HD = 128
FFE = 768
TOP = 8
BLK = 128
DIST = 3
CAP = 16
CHUNKS = (8, 8)
ALL = ("ctx", "head")
BF16 = jnp.bfloat16
F32 = jnp.float32
NT = (((1,), (1,)), ((), ()))
TN = (((0,), (0,)), ((), ()))
EXPONENT = math.log2(math.e) / math.sqrt(HD)


def params(steps=1, limit=56):
    return pltpu.CompilerParams(
        dimension_semantics=("arbitrary",) * steps, vmem_limit_bytes=limit * 1024 * 1024
    )


def held(array):
    return pltpu.with_memory_space_constraint(array, pltpu.VMEM)


def attention_kernel(
    first, stride, shard, head, wanted, q_ref, k_ref, v_ref, far0_ref, far1_ref, far2_ref, weight_ref, *refs
):
    out_refs, (mixed_ref, w_ref, sem) = refs[:-3], refs[-3:]
    step = pl.program_id(0)
    load = pltpu.make_async_copy(weight_ref, w_ref, sem)
    pl.when(step == 0)(load.start)
    steps = len(out_refs)
    blocks = k_ref.shape[0] // BLK
    heads = q_ref.shape[1] // HD
    block = lax.rem(head[0] + first + stride * step, blocks)
    far_refs = (far0_ref, far1_ref, far2_ref)

    def attend(wide):
        rows = lax.broadcasted_iota(jnp.int32, (2 * BLK, BLK), 0)
        columns = lax.broadcasted_iota(jnp.int32, (2 * BLK, BLK), 1)
        bias = jnp.where(rows > columns + lax.rem(block, 2) * BLK, -jnp.inf, 0.0)
        bias = jnp.concatenate([bias] * heads, axis=1)
        reach = [jnp.where(shard[0] >= wanted[0, j], 0.0, -jnp.inf) for j in range(DIST)]
        keys = jnp.concatenate([k_ref[:wide]] + [r[0] for r in far_refs], axis=0)
        values = jnp.concatenate([v_ref[:wide]] + [r[1] for r in far_refs], axis=0)
        query = jnp.concatenate([q_ref[:, n * HD : (n + 1) * HD] for n in range(heads)], axis=0)
        score = lax.dot_general(keys, query, NT, preferred_element_type=F32)
        early = wide - 2 * BLK
        parts = [score[:early]] if early else []
        parts.append(score[early:wide] + bias)
        for j in range(DIST):
            parts.append(score[wide + j * BLK : wide + (j + 1) * BLK] + reach[j])
        score = jnp.concatenate(parts, axis=0)
        highest = jnp.max(score, axis=0, keepdims=True)
        weight = jnp.exp2((score - highest) * EXPONENT)
        denominator = jnp.sum(weight, axis=0, keepdims=True)
        mixed = lax.dot_general(values, weight.astype(BF16), TN, preferred_element_type=F32)
        mixed = mixed / denominator
        for n in range(heads):
            mixed_ref[pl.ds(step * BLK, BLK), n * HD : (n + 1) * HD] = (
                mixed[:, n * BLK : (n + 1) * BLK].T.astype(BF16)
            )

    for pair in range(blocks // 2):
        pl.when(block // 2 == pair)(functools.partial(attend, 2 * BLK * (pair + 1)))

    @pl.when(step == steps - 1)
    def _():
        load.wait()
        for i, out_ref in enumerate(out_refs):
            out_ref[...] = jnp.dot(
                mixed_ref[i * BLK : (i + 1) * BLK], w_ref[...], preferred_element_type=F32
            ).astype(BF16)


def attention(shard, head, wanted, queries, keys, values, far, out_weight, first, stride, steps):
    length, wide = queries.shape
    width = out_weight.shape[1]
    at = lambda i, head: lax.rem(head[0] + first + stride * i, length // BLK)
    whole = lambda shape: pl.BlockSpec(
        shape, lambda i, s, h, w: (0,) * len(shape), pipeline_mode=pl.Buffered(1)
    )
    return pl.pallas_call(
        functools.partial(attention_kernel, first, stride),
        grid_spec=pltpu.PrefetchScalarGridSpec(
            num_scalar_prefetch=3,
            grid=(steps,),
            in_specs=[
                pl.BlockSpec((BLK, wide), lambda i, s, h, w: (at(i, h), 0)),
                whole(keys.shape),
                whole(values.shape),
            ]
            + [pl.BlockSpec((2, BLK, HD), lambda i, s, h, w: (0, at(i, h), 0))] * DIST
            + [pl.BlockSpec(memory_space=pl.ANY)],
            out_specs=(whole((BLK, width)),) * steps,
            scratch_shapes=[
                pltpu.VMEM((steps * BLK, wide), BF16),
                pltpu.VMEM(out_weight.shape, BF16),
                pltpu.SemaphoreType.DMA,
            ],
        ),
        out_shape=(jax.ShapeDtypeStruct((BLK, width), BF16),) * steps,
        compiler_params=params(),
        name="attention",
    )(shard, head, wanted, queries, keys, values, *far, out_weight)


def tables_kernel(routes_ref, weights_ref, *refs):
    top, tokens = routes_ref.shape
    chunks = len(CHUNKS)
    send_refs, table_refs, spread_refs = refs[:chunks], refs[chunks : -chunks], refs[-chunks:]
    experts = spread_refs[0].shape[0]
    names = lax.broadcasted_iota(jnp.int32, (experts, tokens), 0)
    chosen = jnp.zeros((experts, tokens), F32)
    weight = jnp.zeros((experts, tokens), F32)
    for k in range(top):
        here = routes_ref[k : k + 1, :] == names
        chosen = jnp.where(here, 1.0, chosen)
        weight = jnp.where(here, weights_ref[k : k + 1, :], weight)
    before = (
        lax.broadcasted_iota(jnp.int32, (tokens, tokens), 0)
        < lax.broadcasted_iota(jnp.int32, (tokens, tokens), 1)
    ).astype(BF16)
    place = jnp.dot(chosen.astype(BF16), before, preferred_element_type=F32)
    place = jnp.where(chosen > 0.0, place, -1.0)
    high = weight.astype(BF16).astype(F32)
    low = weight - high

    first = 0
    for send_ref, table_ref, spread_ref, slots in zip(
        send_refs, table_refs, spread_refs, CHUNKS
    ):

        def spread(value):
            for s in range(slots):
                spread_ref[:, s, :] = jnp.where(place == float(first + s), value, 0.0)
            return spread_ref[...].reshape(experts * slots, tokens).astype(BF16)

        send_ref[...] = spread(1.0)
        table_ref[:, :tokens] = spread(high)
        table_ref[:, tokens:] = spread(low)
        first += slots


def tables(routes, route_weights, experts):
    tokens = routes.shape[0]
    shapes = lambda columns: tuple(
        jax.ShapeDtypeStruct((experts * slots, columns), BF16) for slots in CHUNKS
    )
    made = pl.pallas_call(
        tables_kernel,
        out_shape=shapes(tokens) + shapes(2 * tokens),
        scratch_shapes=[pltpu.VMEM((experts, slots, tokens), F32) for slots in CHUNKS],
        compiler_params=params(0),
        name="tables",
    )(routes.T, route_weights.T)
    return made[: len(CHUNKS)], made[len(CHUNKS) :]


def norm_kernel(
    own_ref, r1_ref, r2_ref, r3_ref, residual_ref, gain_ref, send_ref, attended_ref, normed_ref, out_ref
):
    @pl.when(pl.program_id(0) == 0)
    def _():
        total = residual_ref[...].astype(F32) + own_ref[...].astype(F32)
        for part_ref in (r1_ref, r2_ref, r3_ref):
            total = total + part_ref[...].astype(F32)
        attended = total.astype(BF16)
        attended_ref[...] = attended
        wide = attended.astype(F32)
        inverse = lax.rsqrt(jnp.mean(wide * wide, axis=1, keepdims=True) + 1e-06)
        normed_ref[...] = (wide * inverse * gain_ref[...]).astype(BF16)

    out_ref[...] = jnp.dot(send_ref[...], normed_ref[...], preferred_element_type=F32).astype(BF16)


def norm_dispatch(own, others, residual, gain, send):
    tokens, width = residual.shape
    rows = send.shape[0]
    step = 512
    whole = lambda shape: pl.BlockSpec(shape, lambda i: (0,) * len(shape))
    return pl.pallas_call(
        norm_kernel,
        grid=(rows // step,),
        in_specs=[whole((tokens, width))]
        + [pl.BlockSpec(memory_space=pltpu.VMEM)] * 3
        + [whole((tokens, width)), whole((1, width)), pl.BlockSpec((step, tokens), lambda i: (i, 0))],
        out_specs=(
            whole((tokens, width)),
            whole((tokens, width)),
            pl.BlockSpec((step, width), lambda i: (i, 0)),
        ),
        out_shape=(
            jax.ShapeDtypeStruct((tokens, width), BF16),
            jax.ShapeDtypeStruct((tokens, width), BF16),
            jax.ShapeDtypeStruct((rows, width), BF16),
        ),
        compiler_params=params(),
        name="norm_dispatch",
    )(own, *others, residual, gain.reshape(1, width), send)


def dispatch_kernel(send_ref, normed_ref, out_ref):
    out_ref[...] = jnp.dot(send_ref[...], normed_ref[...], preferred_element_type=F32).astype(BF16)


def dispatch(send, normed):
    tokens, width = normed.shape
    rows = send.shape[0]
    step = 512
    return pl.pallas_call(
        dispatch_kernel,
        grid=(rows // step,),
        in_specs=[
            pl.BlockSpec((step, tokens), lambda i: (i, 0)),
            pl.BlockSpec((tokens, width), lambda i: (0, 0)),
        ],
        out_specs=pl.BlockSpec((step, width), lambda i: (i, 0)),
        out_shape=jax.ShapeDtypeStruct((rows, width), BF16),
        compiler_params=params(),
        name="dispatch",
    )(send, normed)


def expert_kernel(x_ref, gate_up_ref, down_ref, out_ref):
    projected = jnp.dot(x_ref[...], gate_up_ref[0], preferred_element_type=F32)
    gate, up = projected[:, :FFE], projected[:, FFE:]
    hidden = (gate / (1.0 + jnp.exp(-gate)) * up).astype(BF16)
    out_ref[...] = jnp.dot(hidden, down_ref[0], preferred_element_type=F32).astype(BF16)


def expert(x, gate_up, down):
    rows, width = x.shape
    step = 256
    whole = lambda shape: pl.BlockSpec(
        shape, lambda i: (0,) * len(shape), pipeline_mode=pl.Buffered(1)
    )
    return pl.pallas_call(
        expert_kernel,
        grid=(rows // step,),
        in_specs=[
            pl.BlockSpec((step, width), lambda i: (i, 0)),
            whole(gate_up.shape),
            whole(down.shape),
        ],
        out_specs=pl.BlockSpec((step, width), lambda i: (i, 0)),
        out_shape=jax.ShapeDtypeStruct((rows, width), BF16),
        compiler_params=params(),
        name="expert",
    )(x, gate_up, down)


def combine_kernel(table_ref, rows_ref, *refs):
    before_ref, (out_ref, total_ref) = (refs[0] if len(refs) == 3 else None), refs[-2:]
    step = pl.program_id(0)
    tokens = out_ref.shape[0]
    part = lax.dot_general(table_ref[...], rows_ref[...], TN, preferred_element_type=F32)
    part = part[:tokens] + part[tokens:]

    @pl.when(step == 0)
    def _():
        total_ref[...] = part if before_ref is None else part + before_ref[...]

    @pl.when(step > 0)
    def _():
        total_ref[...] += part

    @pl.when(step == pl.num_programs(0) - 1)
    def _():
        out_ref[...] = total_ref[...].astype(out_ref.dtype)


def combine(table, rows, before, dtype):
    count, width = rows.shape
    tokens = table.shape[1] // 2
    step = 512
    whole = lambda shape: pl.BlockSpec(shape, lambda i: (0,) * len(shape))
    operands = (table, rows) + (() if before is None else (before,))
    return pl.pallas_call(
        combine_kernel,
        grid=(count // step,),
        in_specs=[
            pl.BlockSpec((step, 2 * tokens), lambda i: (i, 0)),
            pl.BlockSpec((step, width), lambda i: (i, 0)),
        ]
        + ([] if before is None else [whole(before.shape)]),
        out_specs=whole((tokens, width)),
        out_shape=jax.ShapeDtypeStruct((tokens, width), dtype),
        scratch_shapes=[pltpu.VMEM((tokens, width), F32)],
        compiler_params=params(),
        name="combine",
    )(*operands)


def fetch(packed, distance):
    shards = lax.axis_size("ctx")

    def back(by, block):
        return lax.ppermute(block, "ctx", [(i, i + by) for i in range(shards - by)])

    return lax.switch(
        distance,
        [lambda block: block] + [functools.partial(back, by) for by in range(1, shards)],
        packed,
    )


def body(
    queries,
    keys,
    values,
    distances,
    out_weight,
    residual,
    norm_gain,
    expert_gate_up,
    expert_down,
    routes,
    route_weights,
):
    tokens, width = residual.shape
    devices = lax.axis_size(ALL)
    me, head = lax.axis_index("ctx"), lax.axis_index("head")
    packed = jnp.stack([keys, values])
    far = [fetch(packed, distances[0, j]) for j in range(DIST)]
    send, table = tables(routes, route_weights, devices)
    group = lax.axis_size("head")

    shard, place = me.reshape(1), head.reshape(1)

    def project(place, first, stride, steps):
        return attention(
            shard, place, distances, queries, keys, values, far, out_weight, first, stride, steps
        )

    def hand(block, by):
        return lax.ppermute(block, "head", [(i, (i + by) % group) for i in range(group)])

    (two,) = project(place, 2, 1, 1)
    two, place = lax.optimization_barrier((two, place))
    two = hand(two, 2)
    one, three = project(place, 1, 2, 2)
    one, three, place = lax.optimization_barrier((one, three, place))
    others = [held(a) for a in (two, hand(one, 1), hand(three, 3))]
    (own,) = project(place, 0, 1, 1)
    attended, normed, first = norm_dispatch(own, others, residual, norm_gain, send[0])
    exchange = lambda a: lax.all_to_all(a, ALL, split_axis=0, concat_axis=0, tiled=True)
    arrived = [exchange(first)] + [exchange(dispatch(s, normed)) for s in send[1:]]
    returned = [exchange(expert(a, expert_gate_up, expert_down)) for a in arrived]
    total = None
    for c, (t, r) in enumerate(zip(table, returned)):
        total = combine(t, r, total, BF16 if c == len(CHUNKS) - 1 else F32)
    return (attended, total)


def solution(mesh):
    return jax.shard_map(
        body,
        mesh=mesh,
        in_specs=(
            P("ctx", "head"),
            P("ctx", "head"),
            P("ctx", "head"),
            P("head", None),
            P("head", None),
            P(ALL, None),
            P(),
            P(ALL, None, None),
            P(ALL, None, None),
            P(ALL, None),
            P(ALL, None),
        ),
        out_specs=(P(ALL, None), P(ALL, None)),
        check_vma=False,
    )
```
